128 devices in a mesh: gx: 8 (over x, core), gy: 16 (over z, y).
Axes of the slice: x: 4, y: 4, z: 4, core: 2. Of those that a mesh axis runs over, the one named last changes fastest.
Arguments:
- features: bfloat16 [64, 128, 96, 128], P('gx', 'gy'), may hold values from -6 to 6
- active_mask: int32 [64, 128, 128], P('gx', 'gy'), may hold values 0 or 1
- owners: int32 [8, 16, 16], P('gx', 'gy'), may hold values from 0 to 15, as said below
- weight: bfloat16 [3, 3, 96, 288], replicated, may hold values from -0.125 to 0.125
- channel_bias: float32 [96], replicated, may hold values from -3 to 3
- cotangent: bfloat16 [8, 512, 96, 512], P('gx', 'gy'), may hold values from -6 to 6
Outputs:
- activations: bfloat16 [8, 512, 96, 512], P('gx', 'gy')
- grad_features: bfloat16 [64, 128, 96, 128], P('gx', 'gy')
- grad_weight: float32 [3, 3, 96, 288], replicated
The draws below stay inside these ranges and needn't reach their ends.
Inputs may be any that keep to these rules, and one draw needn't show every extreme that they name: `owners`: of the bricks of one tile at most 2 have the same owner, and in every gx row one owner receives exactly 2 bricks from every tile of the row.
All inputs are finite; a program needn't handle non-finite values. No bound on the sum of `active_mask` on one device may be relied on, other than what follows from the above.
Results may differ from the reference program's by a relative error of at most 0.005.
Values may be sent and summed in bfloat16 or wider, within the bound.
A program may use at most 320 MiB of HBM per device.

```python
import jax
import jax.numpy as jnp
from jax import lax

C = 96
BY_DEV = 1
BZ = 16
CAP = 2
SLOTS = 32
NX = 64
NY = 128
NZ = 128
NVOX = 1048576
N_GX = 8
N_GY = 16


def draw_owners(key, part):
    bricks_dev = BY_DEV * BZ
    devices = N_GX * N_GY
    key_hot, key_pick, key_order = jax.random.split(key, 3)
    hottest = jax.random.randint(key_hot, (N_GX, 1), 0, N_GY)
    labels = jnp.repeat(jnp.arange(1, N_GY, dtype=jnp.int32), CAP)
    chosen = jax.vmap(lambda subkey: jax.random.permutation(subkey, labels)[:bricks_dev - CAP])(jax.random.split(key_pick, devices))
    offsets = jnp.concatenate([jnp.zeros((devices, CAP), jnp.int32), chosen.astype(jnp.int32)], axis=1)
    offsets = jax.vmap(lambda subkey, listing: jax.random.permutation(subkey, listing))(jax.random.split(key_order, devices), offsets)
    owner_ids = (offsets.reshape(N_GX, N_GY * bricks_dev) + hottest) % N_GY
    return owner_ids.reshape(N_GX, N_GY * BY_DEV, BZ).astype(jnp.int32)


def place_ends(drawn, own_key, low, largest):
    dims = drawn.shape
    index_at = [jax.random.randint(jax.random.fold_in(own_key, axis), (), 0, dims[axis]) for axis in range(len(dims))]
    drawn = drawn.at[tuple(index_at)].set(low)
    longest = dims.index(max(dims))
    index_at[longest] = (index_at[longest] + 1) % dims[longest]
    return drawn.at[tuple(index_at)].set(largest)


def shard_levels(stream_key, dims, shards, low, largest):
    def one(dim, blocks):
        draws = jax.random.uniform(jax.random.fold_in(jax.random.fold_in(stream_key, 6), dim), (blocks,), jnp.float32, low / len(shards), largest / len(shards))
        return jnp.repeat(jnp.exp(draws), dims[dim] // blocks).reshape((-1,) + (1,) * (len(dims) - dim - 1))

    gain = one(*shards[0])
    for cut in shards[1:]:
        gain = gain * one(*cut)
    return gain


def scatter_about(stream_key, dims, scale, limit, cuts=(), kind=jnp.bfloat16):
    values = scale * jax.random.normal(stream_key, dims, jnp.float32)
    if cuts:
        values = values * shard_levels(stream_key, dims, cuts, -0.22, 0.18)
    return jnp.clip(values, -limit, limit).astype(kind)


def setup_inputs(seed: int = 0) -> dict:
    key_list = jax.random.split(jax.random.key(seed), 7)
    features = scatter_about(key_list[0], (NX, NY, C, NZ), 1.0, 6.0, ((0, 8), (1, 16)))
    active_mask = place_ends((jax.random.randint(key_list[1], (NX, NY, NZ), 0, 2) < 1).astype(jnp.int32), jax.random.fold_in(key_list[1], 1), 0, 1)
    owners = draw_owners(jax.random.fold_in(key_list[6], 71), 0)
    weight = scatter_about(key_list[3], (3, 3, C, 3 * C), (27 * C) ** -0.5, 0.125)
    channel_bias = scatter_about(key_list[4], (C,), 0.5, 3.0, (), jnp.float32)
    cotangent = scatter_about(key_list[5], (N_GX, N_GY * SLOTS, C, 512), 1.0, 6.0, ((0, 8), (1, 16)))
    return dict(features=features, active_mask=active_mask, owners=owners, weight=weight, channel_bias=channel_bias, cotangent=cotangent)


FORWARD_SPEC = ("NXYCZ", "XYOZI", "NXYCZ")
BACKWARD_SPEC = ("NXYCZ", "XYIZO", "NXYCZ")


def correlate(volume, kernel, spec):
    result = lax.conv_general_dilated(volume[None].astype(jnp.float32), kernel.astype(jnp.float32), (1, 1, 1), ((1, 1), (1, 1), (1, 1)), dimension_numbers=spec, precision=lax.Precision.HIGHEST)
    return result[0]


def slot_of(owners):
    owner_list = owners.reshape(N_GX, N_GY, BY_DEV * BZ)
    matches = (owner_list[..., None] == jnp.arange(N_GY, dtype=jnp.int32)).astype(jnp.int32)
    before = jnp.cumsum(matches, axis=2) - matches
    ranking = jnp.sum(before * matches, axis=3)
    source = jnp.arange(N_GY, dtype=jnp.int32)[None, :, None]
    return owner_list, (source * CAP + ranking).astype(jnp.int32)


def to_bricks(volume):
    channels = volume.shape[2]
    reshaped = volume.reshape(N_GX, 8, N_GY, BY_DEV, 8, channels, BZ, 8)
    reshaped = jnp.transpose(reshaped, (0, 2, 3, 6, 5, 1, 4, 7))
    return reshaped.reshape(N_GX, N_GY, BY_DEV * BZ, channels, 512)


def from_bricks(bricks):
    channels = bricks.shape[3]
    reshaped = bricks.reshape(N_GX, N_GY, BY_DEV, BZ, channels, 8, 8, 8)
    reshaped = jnp.transpose(reshaped, (0, 5, 1, 2, 6, 4, 3, 7))
    return reshaped.reshape(NX, NY, channels, NZ)


def reference(features, active_mask, owners, weight, channel_bias, cotangent):
    active = active_mask.astype(jnp.float32)[:, :, None, :]
    masked_input = features * active_mask.astype(features.dtype)[:, :, None, :]
    kernel = weight.reshape(3, 3, C, 3, C)
    preact = correlate(masked_input, kernel, FORWARD_SPEC) + channel_bias[None, None, :, None]
    gating = jax.nn.sigmoid(preact)
    activated_scene = (active * preact * gating).astype(jnp.bfloat16)
    owner_list, position = slot_of(owners)
    row_index = jnp.arange(N_GX, dtype=jnp.int32)[:, None, None]
    owner_slots = jnp.zeros((N_GX, N_GY, SLOTS, C, 512), jnp.bfloat16)
    owner_slots = owner_slots.at[row_index, owner_list, position].set(to_bricks(activated_scene))
    activations = owner_slots.reshape(N_GX, N_GY * SLOTS, C, 512)
    cotan_bricks = cotangent.reshape(N_GX, N_GY, SLOTS, C, 512)[row_index, owner_list, position]
    cotangent_scene = from_bricks(cotan_bricks)
    slope = (cotangent_scene.astype(jnp.float32) * active * gating * (1.0 + preact * (1.0 - gating))).astype(jnp.bfloat16)
    mirror = kernel[::-1, ::-1, :, ::-1, :]
    grad_features = (active * correlate(slope, mirror, BACKWARD_SPEC)).astype(jnp.bfloat16)
    flat_slope = jnp.transpose(slope, (2, 0, 1, 3)).reshape(C, NX * NY * NZ).astype(jnp.float32)
    spread = jnp.pad(jnp.transpose(masked_input, (2, 0, 1, 3)).astype(jnp.float32), ((0, 0), (1, 1), (1, 1), (1, 1)))

    def one_tap(offset):
        corner = (jnp.int32(0), (offset // 9).astype(jnp.int32), (offset // 3 % 3).astype(jnp.int32), (offset % 3).astype(jnp.int32))
        window = lax.dynamic_slice(spread, corner, (C, NX, NY, NZ)).reshape(C, NX * NY * NZ)
        return jnp.dot(flat_slope, window.T, precision=lax.Precision.HIGHEST)

    tap_sums = lax.map(one_tap, jnp.arange(27, dtype=jnp.int32))
    grad_weight = jnp.transpose(tap_sums.reshape(3, 3, 3, C, C), (0, 1, 3, 2, 4)).reshape(3, 3, C, 3 * C) * (NVOX ** -0.5)
    return activations, grad_features, grad_weight.astype(jnp.float32)
```

```python
import jax
import jax.numpy as jnp
from jax import lax
from jax.experimental import pallas as pl
from jax.experimental.pallas import tpu as pltpu
from jax.sharding import PartitionSpec as P

C = 96
NX = 8
NY = 8
NZ = 128
GX = 8
GY = 16
SLOTS = 32
K3 = 3 * C
K9 = 9 * C
TOTAL_SCALE = (NX * NY * NZ * GX * GY) ** -0.5
f32 = jnp.float32
bf16 = jnp.bfloat16
MESH = pl.DeviceIdType.MESH

PEERS = (
    (0, 1), (1, 0), (0, 3), (3, 0), (1, 1), (3, 3), (1, 3), (3, 1),
    (0, 2), (2, 0), (2, 1), (1, 2), (2, 3), (3, 2), (2, 2),
)
SIDES = ((1, 0), (-1, 0), (0, 1), (0, -1), (1, 1), (1, -1), (-1, 1), (-1, -1))


def swap_blocks(tiles):
    lane = lax.broadcasted_iota(jnp.int32, tiles[0].shape, 1)
    for step in (8, 4, 2, 1):
        width = step * 8
        upper = (lane // width) % 2 == 1
        moved = list(tiles)
        for i in range(16):
            if i & step:
                continue
            j = i | step
            low, high = tiles[i], tiles[j]
            moved[i] = jnp.where(upper, pltpu.roll(high, width, 1), low)
            moved[j] = jnp.where(upper, high, pltpu.roll(low, NZ - width, 1))
        tiles = moved
    return tiles


def put_stack(stack, x, y, tile, lane):
    zero = jnp.zeros_like(tile)
    stack[x, y, 0:C] = jnp.where(lane == 0, zero, pltpu.roll(tile, 1, 1))
    stack[x, y, C : 2 * C] = tile
    stack[x, y, 2 * C : K3] = jnp.where(lane == NZ - 1, zero, pltpu.roll(tile, NZ - 1, 1))


def conv_step(xi, kernel, stack, acc):
    rows = stack[xi].reshape((NY + 2) * K3, NZ)
    right = jnp.concatenate([rows[K3 * y : K3 * y + K9] for y in range(NY)], axis=1)
    product = jnp.dot(kernel[...], right, preferred_element_type=f32)
    acc[xi + 2] = product[0:C]
    acc[xi + 1] += product[C : 2 * C]
    acc[xi] += product[2 * C : K3]


def body(
    slot_ref, sel_ref, feat, mask, kernel_f, kernel_b, bias, cot_hbm,
    act_hbm, gf_out, gw_out,
    xp, xst, sst, acc, actz, bricks, send, recv, slz, hx, hy, hc, gwacc, red, r1, p1, r2, p3, fin,
    halo_send, halo_recv, shalo_send, shalo_recv, cot_send, cot_recv, act_send, act_recv,
    s1_send, s1_recv, s2_send, s2_recv, s3_send, s3_recv, s4_send, s4_recv, local_sem,
):
    gx = lax.axis_index("gx")
    gy = lax.axis_index("gy")
    gz = gy // 4
    gyy = gy % 4

    def ring_peer(n):
        dz, dy = PEERS[n]
        return ((gz + dz) % 4) * 4 + (gyy + dy) % 4

    def ring_source(n):
        dz, dy = PEERS[n]
        return ((gz + 4 - dz) % 4) * 4 + (gyy + 4 - dy) % 4

    def side(n, sign):
        dx, dy = SIDES[n]
        return ((gx + GX + sign * dx) % GX, (gy + GY + sign * dy) % GY)

    barrier = pltpu.get_barrier_semaphore()
    for n in range(15):
        pl.semaphore_signal(barrier, inc=1, device_id=(gx, ring_peer(n)), device_id_type=MESH)
    for d in range(1, GX):
        pl.semaphore_signal(barrier, inc=1, device_id=((gx + d) % GX, gy), device_id_type=MESH)
    for n in range(4, 8):
        pl.semaphore_signal(barrier, inc=1, device_id=side(n, 1), device_id_type=MESH)

    lane = lax.broadcasted_iota(jnp.int32, (C, NZ), 1)

    def mask_row(x, y):
        return jnp.broadcast_to(mask[x, pl.ds(y, 1)].astype(f32), (C, NZ))

    def masked(x, _):
        for y in range(NY):
            xp[x + 1, y + 1] = (feat[x, y].astype(f32) * mask_row(x, y)).astype(bf16)
        return 0

    lax.fori_loop(0, NX, masked, 0)
    pl.semaphore_wait(barrier, 26)

    def span(d, sign):
        if d == 0:
            return pl.ds(1, 8)
        if sign > 0:
            return 8 if d > 0 else 1
        return 0 if d > 0 else 9

    halos = []
    for n, (dx, dy) in enumerate(SIDES):
        halos.append(
            pltpu.make_async_remote_copy(
                src_ref=xp.at[span(dx, 1), span(dy, 1)],
                dst_ref=xp.at[span(dx, -1), span(dy, -1)],
                send_sem=halo_send.at[n],
                recv_sem=halo_recv.at[n],
                device_id=side(n, 1),
                device_id_type=MESH,
            )
        )
    for copy in halos:
        copy.start()

    def cot_copy(n):
        peer = ring_peer(n)
        return pltpu.make_async_remote_copy(
            src_ref=cot_hbm.at[0, pl.ds(2 * peer, 2)],
            dst_ref=recv.at[pl.ds(2 * gy, 2)],
            send_sem=cot_send.at[n],
            recv_sem=cot_recv.at[n],
            device_id=(gx, peer),
            device_id_type=MESH,
        )

    cots = [cot_copy(n) for n in range(15)]
    for copy in cots:
        copy.start()
    own_cot = pltpu.make_async_copy(
        cot_hbm.at[0, pl.ds(2 * gy, 2)], recv.at[pl.ds(2 * gy, 2)], local_sem.at[0]
    )
    own_cot.start()

    def stack_inner(x, _):
        for y in range(NY):
            put_stack(xst, x + 1, y + 1, xp[x + 1, y + 1], lane)
        return 0

    lax.fori_loop(0, NX, stack_inner, 0)
    for copy in halos:
        copy.wait()

    first_x = (gx > 0).astype(f32)
    last_x = (gx < GX - 1).astype(f32)
    first_y = (gy > 0).astype(f32)
    last_y = (gy < GY - 1).astype(f32)

    def keep(tile, flag):
        return (tile.astype(f32) * flag).astype(bf16)

    def stack_y(x, _):
        put_stack(xst, x, 0, keep(xp[x, 0], first_y), lane)
        put_stack(xst, x, 9, keep(xp[x, 9], last_y), lane)
        return 0

    lax.fori_loop(1, 9, stack_y, 0)

    def stack_x(y, _):
        put_stack(xst, 0, y, keep(xp[0, y], first_x), lane)
        put_stack(xst, 9, y, keep(xp[9, y], last_x), lane)
        return 0

    lax.fori_loop(1, 9, stack_x, 0)
    for x, y, flag in (
        (0, 0, first_x * first_y), (0, 9, first_x * last_y),
        (9, 0, last_x * first_y), (9, 9, last_x * last_y),
    ):
        put_stack(xst, x, y, keep(xp[x, y], flag), lane)

    acc[0] = jnp.zeros((C, NY * NZ), f32)
    acc[1] = jnp.zeros((C, NY * NZ), f32)

    def forward(xi, _):
        conv_step(xi, kernel_f, xst, acc)
        return 0

    lax.fori_loop(0, NX + 2, forward, 0)

    shift = jnp.broadcast_to(bias[...], (C, NZ))

    def activate(x, _):
        for y in range(NY):
            cols = slice(NZ * y, NZ * y + NZ)
            pre = acc[x + 2, :, cols] + shift
            gate = jax.nn.sigmoid(pre)
            on = mask_row(x, y)
            actz[x, :, cols] = (on * pre * gate).astype(bf16)
            acc[x + 2, :, cols] = on * gate * (1.0 + pre * (1.0 - gate))
        return 0

    lax.fori_loop(0, NX, activate, 0)
    bricks[16] = jnp.zeros((C, 512), bf16)

    def to_bricks(n, _):
        u2 = n // 2
        rows = pl.ds(pl.multiple_of((n % 2) * 48, 48), 48)
        cols = pl.ds(pl.multiple_of(u2 * NZ, NZ), NZ)
        tiles = [actz[2 * u2 + j // 8, rows, (j % 8) * NZ : (j % 8) * NZ + NZ] for j in range(16)]
        for z, tile in enumerate(swap_blocks(tiles)):
            bricks[z, rows, cols] = tile
        return 0

    lax.fori_loop(0, 8, to_bricks, 0)

    def fill(s, _):
        send[s] = bricks[sel_ref[s]]
        return 0

    lax.fori_loop(0, SLOTS, fill, 0)

    for n in range(2):
        slz[n] = jnp.zeros((C, NY * NZ), bf16)
        slz[10 + n] = jnp.zeros((C, NY * NZ), bf16)

    own_cot.wait()
    for copy in cots:
        copy.wait()

    def to_slope(n, _):
        u2 = n // 2
        rows = pl.ds(pl.multiple_of((n % 2) * 48, 48), 48)
        cols = pl.ds(pl.multiple_of(u2 * NZ, NZ), NZ)
        tiles = [recv[slot_ref[z], rows, cols] for z in range(16)]
        for j, tile in enumerate(swap_blocks(tiles)):
            part = slice((j % 8) * NZ, (j % 8) * NZ + NZ)
            row = 2 * u2 + j // 8 + 2
            slz[row, rows, part] = (tile.astype(f32) * acc[row, rows, part]).astype(bf16)
        return 0

    lax.fori_loop(0, 8, to_slope, 0)

    def edge(d):
        return 9 if d > 0 else 2

    def strip(d):
        return pl.ds(7 * NZ, NZ) if d > 0 else pl.ds(0, NZ)

    def low(d):
        return 0 if d > 0 else 1

    slope_halos = []
    for n, (dx, dy) in enumerate(SIDES):
        if dy == 0:
            source, target = slz.at[edge(dx)], hx.at[low(dx)]
        elif dx == 0:
            source, target = slz.at[pl.ds(2, 8), :, strip(dy)], hy.at[low(dy)]
        else:
            source, target = slz.at[edge(dx), :, strip(dy)], hc.at[2 * low(dx) + low(dy)]
        slope_halos.append(
            pltpu.make_async_remote_copy(
                src_ref=source,
                dst_ref=target,
                send_sem=shalo_send.at[n],
                recv_sem=shalo_recv.at[n],
                device_id=side(n, 1),
                device_id_type=MESH,
            )
        )
    for copy in slope_halos:
        copy.start()

    def act_copy(n):
        peer = ring_peer(n)
        return pltpu.make_async_remote_copy(
            src_ref=send.at[pl.ds(2 * peer, 2)],
            dst_ref=act_hbm.at[0, pl.ds(2 * gy, 2)],
            send_sem=act_send.at[n],
            recv_sem=act_recv.at[n],
            device_id=(gx, peer),
            device_id_type=MESH,
        )

    acts = [act_copy(n) for n in range(15)]
    for copy in acts:
        copy.start()
    own_act = pltpu.make_async_copy(
        send.at[pl.ds(2 * gy, 2)], act_hbm.at[0, pl.ds(2 * gy, 2)], local_sem.at[1]
    )
    own_act.start()

    gwacc[...] = jnp.zeros((K3, 7 * NZ), f32)

    def weight_terms(xi, _):
        left = jnp.concatenate([slz[xi + 2], slz[xi + 1], slz[xi]], axis=0)
        rows = xst[xi].reshape((NY + 2) * K3, NZ)
        right = jnp.concatenate([rows[K3 * y : K3 * y + K9] for y in range(NY)], axis=1)
        gwacc[:, 0:K9] += lax.dot_general(
            left, right, (((1,), (1,)), ((), ())), preferred_element_type=f32
        )
        return 0

    lax.fori_loop(0, NX + 2, weight_terms, 0)
    for j in range(7):
        red[K3 * j : K3 * j + K3] = gwacc[:, NZ * j : NZ * j + NZ]
    red[7 * K3 : 2048] = jnp.zeros((2048 - 7 * K3, NZ), f32)

    def stage1(d):
        peer = (gx + d) % GX
        return pltpu.make_async_remote_copy(
            src_ref=red.at[pl.ds(256 * peer, 256)],
            dst_ref=r1.at[gx],
            send_sem=s1_send.at[d],
            recv_sem=s1_recv.at[d],
            device_id=(peer, gy),
            device_id_type=MESH,
        )

    ones = [stage1(d) for d in range(1, GX)]
    for copy in ones:
        copy.start()

    def slope_inner(x, _):
        for y in range(NY):
            put_stack(sst, x + 1, y + 1, slz[x + 2, :, NZ * y : NZ * y + NZ], lane)
        return 0

    lax.fori_loop(0, NX, slope_inner, 0)
    for copy in slope_halos:
        copy.wait()

    def slope_y(x, _):
        put_stack(sst, x + 1, 0, keep(hy[0, x], first_y), lane)
        put_stack(sst, x + 1, 9, keep(hy[1, x], last_y), lane)
        return 0

    lax.fori_loop(0, NX, slope_y, 0)
    for y in range(NY):
        cols = slice(NZ * y, NZ * y + NZ)
        put_stack(sst, 0, y + 1, keep(hx[0, :, cols], first_x), lane)
        put_stack(sst, 9, y + 1, keep(hx[1, :, cols], last_x), lane)
    for n, x, y, flag in (
        (0, 0, 0, first_x * first_y), (1, 0, 9, first_x * last_y),
        (2, 9, 0, last_x * first_y), (3, 9, 9, last_x * last_y),
    ):
        put_stack(sst, x, y, keep(hc[n], flag), lane)

    for copy in ones:
        copy.wait()
    total = red[pl.ds(pl.multiple_of(256 * gx, 256), 256)]
    for d in range(1, GX):
        total = total + r1[(gx + GX - d) % GX]
    p1[...] = total

    def stage2(n):
        peer = ring_peer(n)
        return pltpu.make_async_remote_copy(
            src_ref=p1.at[pl.ds(16 * peer, 16)],
            dst_ref=r2.at[gy],
            send_sem=s2_send.at[n],
            recv_sem=s2_recv.at[n],
            device_id=(gx, peer),
            device_id_type=MESH,
        )

    twos = [stage2(n) for n in range(15)]
    for copy in twos:
        copy.start()

    def backward(xi, _):
        conv_step(xi, kernel_b, sst, acc)
        return 0

    lax.fori_loop(0, 4, backward, 0)

    for copy in twos:
        copy.wait()
    part = p1[pl.ds(pl.multiple_of(16 * gy, 16), 16)]
    for n in range(15):
        part = part + r2[ring_source(n)]
    mine = pl.ds(pl.multiple_of(16 * gy, 16), 16)
    p3[mine] = part * TOTAL_SCALE

    def stage3(n):
        return pltpu.make_async_remote_copy(
            src_ref=p3.at[mine],
            dst_ref=p3.at[mine],
            send_sem=s3_send.at[n],
            recv_sem=s3_recv.at[n],
            device_id=(gx, ring_peer(n)),
            device_id_type=MESH,
        )

    threes = [stage3(n) for n in range(15)]
    for copy in threes:
        copy.start()
    lax.fori_loop(4, 7, backward, 0)
    for copy in threes:
        copy.wait()

    block = pl.ds(pl.multiple_of(256 * gx, 256), 256)

    def stage4(d):
        return pltpu.make_async_remote_copy(
            src_ref=p3,
            dst_ref=fin.at[block],
            send_sem=s4_send.at[d],
            recv_sem=s4_recv.at[d],
            device_id=((gx + d) % GX, gy),
            device_id_type=MESH,
        )

    fours = [stage4(d) for d in range(1, GX)]
    for copy in fours:
        copy.start()
    fin[block] = p3[...]
    lax.fori_loop(7, NX + 2, backward, 0)

    def finish(x, _):
        for y in range(NY):
            gf_out[x, y] = (mask_row(x, y) * acc[x + 2, :, NZ * y : NZ * y + NZ]).astype(bf16)
        return 0

    lax.fori_loop(0, NX, finish, 0)
    for copy in fours:
        copy.wait()
    gw_out[...] = fin[...]
    own_act.wait()
    for copy in acts:
        copy.wait()


def routes(owners):
    owner = owners.reshape(-1)
    count = owner.size
    index = jnp.arange(count, dtype=jnp.int32)
    same = owner[:, None] == owner[None, :]
    before = jnp.sum((same & (index[None, :] < index[:, None])).astype(jnp.int32), axis=1)
    slot = owner * 2 + before
    hit = slot[:, None] == jnp.arange(SLOTS, dtype=jnp.int32)[None, :]
    sel = count + jnp.sum(jnp.where(hit, index[:, None] - count, 0), axis=0)
    return slot.astype(jnp.int32), sel.astype(jnp.int32)


def on_device(features, active_mask, owners, weight, channel_bias, cotangent):
    slot, sel = routes(owners)
    taps = weight.reshape(3, 3, C, 3, C)
    kernel_f = jnp.transpose(taps, (0, 2, 1, 3, 4)).reshape(K3, K9)
    kernel_b = jnp.transpose(taps[::-1, ::-1, :, ::-1, :], (0, 4, 1, 3, 2)).reshape(K3, K9)
    smem = pl.BlockSpec(memory_space=pltpu.SMEM)
    vmem = pl.BlockSpec(memory_space=pltpu.VMEM)
    hbm = pl.BlockSpec(memory_space=pl.ANY)
    dma = pltpu.SemaphoreType.DMA
    activations, grad_features, grad = pl.pallas_call(
        body,
        out_shape=(
            jax.ShapeDtypeStruct((1, SLOTS, C, 512), bf16),
            jax.ShapeDtypeStruct((NX, NY, C, NZ), bf16),
            jax.ShapeDtypeStruct((2048, NZ), f32),
        ),
        in_specs=[smem, smem, vmem, vmem, vmem, vmem, vmem, hbm],
        out_specs=(hbm, vmem, vmem),
        scratch_shapes=[
            pltpu.VMEM((NX + 2, NY + 2, C, NZ), bf16),
            pltpu.VMEM((NX + 2, NY + 2, K3, NZ), bf16),
            pltpu.VMEM((NX + 2, NY + 2, K3, NZ), bf16),
            pltpu.VMEM((NX + 4, C, NY * NZ), f32),
            pltpu.VMEM((NX, C, NY * NZ), bf16),
            pltpu.VMEM((17, C, 512), bf16),
            pltpu.VMEM((SLOTS, C, 512), bf16),
            pltpu.VMEM((SLOTS, C, 512), bf16),
            pltpu.VMEM((NX + 4, C, NY * NZ), bf16),
            pltpu.VMEM((2, C, NY * NZ), bf16),
            pltpu.VMEM((2, NX, C, NZ), bf16),
            pltpu.VMEM((4, C, NZ), bf16),
            pltpu.VMEM((K3, 7 * NZ), f32),
            pltpu.VMEM((2048, NZ), f32),
            pltpu.VMEM((GX, 256, NZ), f32),
            pltpu.VMEM((256, NZ), f32),
            pltpu.VMEM((GY, 16, NZ), f32),
            pltpu.VMEM((256, NZ), f32),
            pltpu.VMEM((2048, NZ), f32),
            dma((8,)), dma((8,)), dma((8,)), dma((8,)),
            dma((15,)), dma((15,)), dma((15,)), dma((15,)),
            dma((GX,)), dma((GX,)), dma((15,)), dma((15,)),
            dma((15,)), dma((15,)), dma((GX,)), dma((GX,)),
            dma((2,)),
        ],
        compiler_params=pltpu.CompilerParams(
            collective_id=0, has_side_effects=True, vmem_limit_bytes=60 * 1024 * 1024
        ),
    )(slot, sel, features, active_mask, kernel_f, kernel_b, channel_bias.reshape(C, 1), cotangent)
    grad = jnp.transpose(grad[: 7 * K3].reshape(7, K3, NZ), (1, 0, 2)).reshape(K3, 7 * NZ)
    grad = grad[:, :K9].reshape(3, C, 3, K3)
    return activations, grad_features, jnp.transpose(grad, (0, 2, 1, 3))


def solution(mesh):
    in_specs = (
        P("gx", "gy", None, None),
        P("gx", "gy", None),
        P("gx", "gy", None),
        P(),
        P(),
        P("gx", "gy", None, None),
    )
    out_specs = (P("gx", "gy", None, None), P("gx", "gy", None, None), P())
    return jax.shard_map(
        on_device, mesh=mesh, in_specs=in_specs, out_specs=out_specs, check_vma=False
    )
```

```python
import jax
import jax.numpy as jnp
from jax import lax
from jax.experimental import pallas as pl
from jax.experimental.pallas import tpu as pltpu
from jax.sharding import PartitionSpec as P

C = 96
NX = 8
NY = 8
NZ = 128
GX = 8
GY = 16
SLOTS = 32
K3 = 3 * C
K9 = 9 * C
TOTAL_SCALE = (NX * NY * NZ * GX * GY) ** -0.5
f32 = jnp.float32
bf16 = jnp.bfloat16
MESH = pl.DeviceIdType.MESH

PEERS = (
    (0, 1), (1, 0), (0, 3), (3, 0), (1, 1), (3, 3), (1, 3), (3, 1),
    (0, 2), (2, 0), (2, 1), (1, 2), (2, 3), (3, 2), (2, 2),
)
SIDES = ((1, 0), (-1, 0), (0, 1), (0, -1), (1, 1), (1, -1), (-1, 1), (-1, -1))


def swap_blocks(tiles):
    lane = lax.broadcasted_iota(jnp.int32, tiles[0].shape, 1)
    for step in (8, 4, 2, 1):
        width = step * 8
        upper = (lane // width) % 2 == 1
        moved = list(tiles)
        for i in range(16):
            if i & step:
                continue
            j = i | step
            low, high = tiles[i], tiles[j]
            moved[i] = jnp.where(upper, pltpu.roll(high, width, 1), low)
            moved[j] = jnp.where(upper, high, pltpu.roll(low, NZ - width, 1))
        tiles = moved
    return tiles


def put_stack(stack, x, y, tile, lane):
    zero = jnp.zeros_like(tile)
    stack[x, y, 0:C] = jnp.where(lane == 0, zero, pltpu.roll(tile, 1, 1))
    stack[x, y, C : 2 * C] = tile
    stack[x, y, 2 * C : K3] = jnp.where(lane == NZ - 1, zero, pltpu.roll(tile, NZ - 1, 1))


def conv_step(xi, kernel, stack, acc):
    rows = stack[xi].reshape((NY + 2) * K3, NZ)
    right = jnp.concatenate([rows[K3 * y : K3 * y + K9] for y in range(NY)], axis=1)
    product = jnp.dot(kernel[...], right, preferred_element_type=f32)
    acc[xi + 2] = product[0:C]
    acc[xi + 1] += product[C : 2 * C]
    acc[xi] += product[2 * C : K3]


def body(
    owners, feat, mask, weight, bias, cot_hbm,
    act_hbm, gf_out, gw_out,
    kernel_f, kernel_b, xp, xst, sst, acc, actz, bricks, send, recv, slz, hx, hy, hc, gwacc, red, r1, p1, r2, p3, fin,
    halo_send, halo_recv, shalo_send, shalo_recv, cot_send, cot_recv, act_send, act_recv,
    s1_send, s1_recv, s2_send, s2_recv, s3_send, s3_recv, s4_send, s4_recv, local_sem,
):
    gx = lax.axis_index("gx")
    gy = lax.axis_index("gy")
    gz = gy // 4
    gyy = gy % 4

    def ring_peer(n):
        dz, dy = PEERS[n]
        return ((gz + dz) % 4) * 4 + (gyy + dy) % 4

    def ring_source(n):
        dz, dy = PEERS[n]
        return ((gz + 4 - dz) % 4) * 4 + (gyy + 4 - dy) % 4

    def side(n, sign):
        dx, dy = SIDES[n]
        return ((gx + GX + sign * dx) % GX, (gy + GY + sign * dy) % GY)

    barrier = pltpu.get_barrier_semaphore()
    for n in range(15):
        pl.semaphore_signal(barrier, inc=1, device_id=(gx, ring_peer(n)), device_id_type=MESH)
    for d in range(1, GX):
        pl.semaphore_signal(barrier, inc=1, device_id=((gx + d) % GX, gy), device_id_type=MESH)
    for n in range(4, 8):
        pl.semaphore_signal(barrier, inc=1, device_id=side(n, 1), device_id_type=MESH)

    lane = lax.broadcasted_iota(jnp.int32, (C, NZ), 1)

    def mask_row(x, y):
        return jnp.broadcast_to(mask[x, pl.ds(y, 1)].astype(f32), (C, NZ))

    def masked(x, _):
        for y in range(NY):
            xp[x + 1, y + 1] = (feat[x, y].astype(f32) * mask_row(x, y)).astype(bf16)
        return 0

    lax.fori_loop(0, NX, masked, 0)
    pl.semaphore_wait(barrier, 26)

    def span(d, sign):
        if d == 0:
            return pl.ds(1, 8)
        if sign > 0:
            return 8 if d > 0 else 1
        return 0 if d > 0 else 9

    halos = []
    for n, (dx, dy) in enumerate(SIDES):
        halos.append(
            pltpu.make_async_remote_copy(
                src_ref=xp.at[span(dx, 1), span(dy, 1)],
                dst_ref=xp.at[span(dx, -1), span(dy, -1)],
                send_sem=halo_send.at[n],
                recv_sem=halo_recv.at[n],
                device_id=side(n, 1),
                device_id_type=MESH,
            )
        )
    for copy in halos:
        copy.start()

    def cot_copy(n, k):
        peer = ring_peer(n)
        return pltpu.make_async_remote_copy(
            src_ref=cot_hbm.at[0, 2 * peer + k],
            dst_ref=recv.at[2 * gy + k],
            send_sem=cot_send.at[15 * k + n],
            recv_sem=cot_recv.at[15 * k + n],
            device_id=(gx, peer),
            device_id_type=MESH,
        )

    cots = [cot_copy(n, k) for k in range(2) for n in range(15)]
    for copy in cots:
        copy.start()
    own_cot = pltpu.make_async_copy(
        cot_hbm.at[0, pl.ds(2 * gy, 2)], recv.at[pl.ds(2 * gy, 2)], local_sem.at[0]
    )
    own_cot.start()

    for a in range(3):
        kernel_f[C * a : C * a + C] = jnp.concatenate([weight[a, b] for b in range(3)], axis=1)
        blocks = []
        for b in range(3):
            turned = jnp.transpose(weight[2 - a, 2 - b].astype(f32))
            for c in range(3):
                blocks.append(turned[(2 - c) * C : (3 - c) * C].astype(bf16))
        kernel_b[C * a : C * a + C] = jnp.concatenate(blocks, axis=1)

    owner = [owners[0, 0, z] for z in range(16)]
    slots = []
    for z in range(16):
        rank = jnp.int32(0)
        for before in range(z):
            rank = rank + (owner[before] == owner[z]).astype(jnp.int32)
        slots.append(2 * owner[z] + rank)

    def stack_inner(x, _):
        for y in range(NY):
            put_stack(xst, x + 1, y + 1, xp[x + 1, y + 1], lane)
        return 0

    lax.fori_loop(0, NX, stack_inner, 0)
    for copy in halos:
        copy.wait()

    first_x = (gx > 0).astype(f32)
    last_x = (gx < GX - 1).astype(f32)
    first_y = (gy > 0).astype(f32)
    last_y = (gy < GY - 1).astype(f32)

    def keep(tile, flag):
        return (tile.astype(f32) * flag).astype(bf16)

    def stack_y(x, _):
        put_stack(xst, x, 0, keep(xp[x, 0], first_y), lane)
        put_stack(xst, x, 9, keep(xp[x, 9], last_y), lane)
        return 0

    lax.fori_loop(1, 9, stack_y, 0)

    def stack_x(y, _):
        put_stack(xst, 0, y, keep(xp[0, y], first_x), lane)
        put_stack(xst, 9, y, keep(xp[9, y], last_x), lane)
        return 0

    lax.fori_loop(1, 9, stack_x, 0)
    for x, y, flag in (
        (0, 0, first_x * first_y), (0, 9, first_x * last_y),
        (9, 0, last_x * first_y), (9, 9, last_x * last_y),
    ):
        put_stack(xst, x, y, keep(xp[x, y], flag), lane)

    acc[0] = jnp.zeros((C, NY * NZ), f32)
    acc[1] = jnp.zeros((C, NY * NZ), f32)

    def forward(xi, _):
        conv_step(xi, kernel_f, xst, acc)
        return 0

    lax.fori_loop(0, NX + 2, forward, 0)

    shift = jnp.transpose(jnp.broadcast_to(bias[...], (NZ, C)))

    def activate(x, _):
        for y in range(NY):
            cols = slice(NZ * y, NZ * y + NZ)
            pre = acc[x + 2, :, cols] + shift
            gate = jax.nn.sigmoid(pre)
            on = mask_row(x, y)
            actz[x, :, cols] = (on * pre * gate).astype(bf16)
            acc[x + 2, :, cols] = on * gate * (1.0 + pre * (1.0 - gate))
        return 0

    lax.fori_loop(0, NX, activate, 0)
    bricks[16] = jnp.zeros((C, 512), bf16)

    def to_bricks(n, _):
        u2 = n // 2
        rows = pl.ds(pl.multiple_of((n % 2) * 48, 48), 48)
        cols = pl.ds(pl.multiple_of(u2 * NZ, NZ), NZ)
        tiles = [actz[2 * u2 + j // 8, rows, (j % 8) * NZ : (j % 8) * NZ + NZ] for j in range(16)]
        for z, tile in enumerate(swap_blocks(tiles)):
            bricks[z, rows, cols] = tile
        return 0

    lax.fori_loop(0, 8, to_bricks, 0)

    def fill(s, _):
        brick = jnp.int32(16)
        for z in range(16):
            brick = jnp.where(slots[z] == s, z, brick)
        send[s] = bricks[brick]
        return 0

    lax.fori_loop(0, SLOTS, fill, 0)

    for n in range(2):
        slz[n] = jnp.zeros((C, NY * NZ), bf16)
        slz[10 + n] = jnp.zeros((C, NY * NZ), bf16)

    own_cot.wait()
    for copy in cots:
        copy.wait()

    def act_copy(n, k):
        peer = ring_peer(n)
        return pltpu.make_async_remote_copy(
            src_ref=send.at[2 * peer + k],
            dst_ref=act_hbm.at[0, 2 * gy + k],
            send_sem=act_send.at[15 * k + n],
            recv_sem=act_recv.at[15 * k + n],
            device_id=(gx, peer),
            device_id_type=MESH,
        )

    acts = [act_copy(n, k) for k in range(2) for n in range(15)]
    own_act = pltpu.make_async_copy(
        send.at[pl.ds(2 * gy, 2)], act_hbm.at[0, pl.ds(2 * gy, 2)], local_sem.at[1]
    )
    own_act.start()
    for copy in acts[:4]:
        copy.start()

    def to_slope(n, _):
        u2 = n // 2
        rows = pl.ds(pl.multiple_of((n % 2) * 48, 48), 48)
        cols = pl.ds(pl.multiple_of(u2 * NZ, NZ), NZ)
        tiles = [recv[slots[z], rows, cols] for z in range(16)]
        for j, tile in enumerate(swap_blocks(tiles)):
            part = slice((j % 8) * NZ, (j % 8) * NZ + NZ)
            row = 2 * u2 + j // 8 + 2
            slz[row, rows, part] = (tile.astype(f32) * acc[row, rows, part]).astype(bf16)
        return 0

    lax.fori_loop(0, 8, to_slope, 0)

    def edge(d):
        return 9 if d > 0 else 2

    def strip(d):
        return pl.ds(7 * NZ, NZ) if d > 0 else pl.ds(0, NZ)

    def low(d):
        return 0 if d > 0 else 1

    slope_halos = []
    for n, (dx, dy) in enumerate(SIDES):
        if dy == 0:
            source, target = slz.at[edge(dx)], hx.at[low(dx)]
        elif dx == 0:
            source, target = slz.at[pl.ds(2, 8), :, strip(dy)], hy.at[low(dy)]
        else:
            source, target = slz.at[edge(dx), :, strip(dy)], hc.at[2 * low(dx) + low(dy)]
        slope_halos.append(
            pltpu.make_async_remote_copy(
                src_ref=source,
                dst_ref=target,
                send_sem=shalo_send.at[n],
                recv_sem=shalo_recv.at[n],
                device_id=side(n, 1),
                device_id_type=MESH,
            )
        )
    for copy in slope_halos:
        copy.start()
    for copy in acts[4:15]:
        copy.start()

    gwacc[...] = jnp.zeros((K3, 7 * NZ), f32)

    def weight_terms(xi, _):
        left = jnp.concatenate([slz[xi + 2], slz[xi + 1], slz[xi]], axis=0)
        rows = xst[xi].reshape((NY + 2) * K3, NZ)
        right = jnp.concatenate([rows[K3 * y : K3 * y + K9] for y in range(NY)], axis=1)
        gwacc[:, 0:K9] += lax.dot_general(
            left, right, (((1,), (1,)), ((), ())), preferred_element_type=f32
        )
        return 0

    lax.fori_loop(0, NX + 2, weight_terms, 0)
    for j in range(7):
        red[K3 * j : K3 * j + K3] = gwacc[:, NZ * j : NZ * j + NZ]
    red[7 * K3 : 2048] = jnp.zeros((2048 - 7 * K3, NZ), f32)

    def stage1(d):
        peer = (gx + d) % GX
        return pltpu.make_async_remote_copy(
            src_ref=red.at[pl.ds(256 * peer, 256)],
            dst_ref=r1.at[gx],
            send_sem=s1_send.at[d],
            recv_sem=s1_recv.at[d],
            device_id=(peer, gy),
            device_id_type=MESH,
        )

    ones = [stage1(d) for d in range(1, GX)]
    for copy in ones:
        copy.start()

    def slope_inner(x, _):
        for y in range(NY):
            put_stack(sst, x + 1, y + 1, slz[x + 2, :, NZ * y : NZ * y + NZ], lane)
        return 0

    lax.fori_loop(0, NX, slope_inner, 0)
    for copy in slope_halos:
        copy.wait()

    def slope_y(x, _):
        put_stack(sst, x + 1, 0, keep(hy[0, x], first_y), lane)
        put_stack(sst, x + 1, 9, keep(hy[1, x], last_y), lane)
        return 0

    lax.fori_loop(0, NX, slope_y, 0)
    for y in range(NY):
        cols = slice(NZ * y, NZ * y + NZ)
        put_stack(sst, 0, y + 1, keep(hx[0, :, cols], first_x), lane)
        put_stack(sst, 9, y + 1, keep(hx[1, :, cols], last_x), lane)
    for n, x, y, flag in (
        (0, 0, 0, first_x * first_y), (1, 0, 9, first_x * last_y),
        (2, 9, 0, last_x * first_y), (3, 9, 9, last_x * last_y),
    ):
        put_stack(sst, x, y, keep(hc[n], flag), lane)

    for copy in ones:
        copy.wait()
    total = red[pl.ds(pl.multiple_of(256 * gx, 256), 256)]
    for d in range(1, GX):
        total = total + r1[(gx + GX - d) % GX]
    p1[...] = total

    def stage2(n):
        peer = ring_peer(n)
        return pltpu.make_async_remote_copy(
            src_ref=p1.at[pl.ds(16 * peer, 16)],
            dst_ref=r2.at[gy],
            send_sem=s2_send.at[n],
            recv_sem=s2_recv.at[n],
            device_id=(gx, peer),
            device_id_type=MESH,
        )

    twos = [stage2(n) for n in range(15)]
    for copy in twos:
        copy.start()
    for copy in acts[15:18]:
        copy.start()

    def backward(xi, _):
        conv_step(xi, kernel_b, sst, acc)
        return 0

    lax.fori_loop(0, 4, backward, 0)

    for copy in twos:
        copy.wait()
    part = p1[pl.ds(pl.multiple_of(16 * gy, 16), 16)]
    for n in range(15):
        part = part + r2[ring_source(n)]
    mine = pl.ds(pl.multiple_of(16 * gy, 16), 16)
    p3[mine] = part * TOTAL_SCALE

    def stage3(n):
        return pltpu.make_async_remote_copy(
            src_ref=p3.at[mine],
            dst_ref=p3.at[mine],
            send_sem=s3_send.at[n],
            recv_sem=s3_recv.at[n],
            device_id=(gx, ring_peer(n)),
            device_id_type=MESH,
        )

    threes = [stage3(n) for n in range(15)]
    for copy in threes:
        copy.start()
    for copy in acts[18:]:
        copy.start()
    lax.fori_loop(4, 7, backward, 0)
    for copy in threes:
        copy.wait()

    block = pl.ds(pl.multiple_of(256 * gx, 256), 256)

    def stage4(d):
        return pltpu.make_async_remote_copy(
            src_ref=p3,
            dst_ref=fin.at[block],
            send_sem=s4_send.at[d],
            recv_sem=s4_recv.at[d],
            device_id=((gx + d) % GX, gy),
            device_id_type=MESH,
        )

    fours = [stage4(d) for d in range(1, GX)]
    for copy in fours:
        copy.start()
    fin[block] = p3[...]
    lax.fori_loop(7, NX + 2, backward, 0)

    def finish(x, _):
        for y in range(NY):
            gf_out[x, y] = (mask_row(x, y) * acc[x + 2, :, NZ * y : NZ * y + NZ]).astype(bf16)
        return 0

    lax.fori_loop(0, NX, finish, 0)
    for copy in fours:
        copy.wait()
    full = jnp.concatenate([fin[K3 * j : K3 * j + K3] for j in range(7)], axis=1)
    for a in range(3):
        for b in range(3):
            gw_out[a, b] = full[C * a : C * a + C, K3 * b : K3 * b + K3]
    own_act.wait()
    for copy in acts:
        copy.wait()


def hand_over(act, gf, gw, act_out, gf_out, gw_out, sems):
    copies = []
    for n in range(8):
        part = pl.ds(4 * n, 4)
        copies.append(pltpu.make_async_copy(act.at[0, part], act_out.at[0, part], sems.at[n]))
    for n in range(4):
        part = pl.ds(2 * n, 2)
        copies.append(pltpu.make_async_copy(gf.at[part], gf_out.at[part], sems.at[8 + n]))
    for n in range(3):
        copies.append(pltpu.make_async_copy(gw.at[n], gw_out.at[n], sems.at[12 + n]))
    for copy in copies:
        copy.start()
    for copy in copies:
        copy.wait()


def on_device(features, active_mask, owners, weight, channel_bias, cotangent):
    smem = pl.BlockSpec(memory_space=pltpu.SMEM)
    vmem = pl.BlockSpec(memory_space=pltpu.VMEM)
    hbm = pl.BlockSpec(memory_space=pl.ANY)
    dma = pltpu.SemaphoreType.DMA
    activations, grad_features, grad = pl.pallas_call(
        body,
        out_shape=(
            jax.ShapeDtypeStruct((1, SLOTS, C, 512), bf16),
            jax.ShapeDtypeStruct((NX, NY, C, NZ), bf16),
            jax.ShapeDtypeStruct((3, 3, C, K3), f32),
        ),
        in_specs=[smem, vmem, vmem, vmem, vmem, hbm],
        out_specs=(hbm, vmem, vmem),
        scratch_shapes=[
            pltpu.VMEM((K3, K9), bf16),
            pltpu.VMEM((K3, K9), bf16),
            pltpu.VMEM((NX + 2, NY + 2, C, NZ), bf16),
            pltpu.VMEM((NX + 2, NY + 2, K3, NZ), bf16),
            pltpu.VMEM((NX + 2, NY + 2, K3, NZ), bf16),
            pltpu.VMEM((NX + 4, C, NY * NZ), f32),
            pltpu.VMEM((NX, C, NY * NZ), bf16),
            pltpu.VMEM((17, C, 512), bf16),
            pltpu.VMEM((SLOTS, C, 512), bf16),
            pltpu.VMEM((SLOTS, C, 512), bf16),
            pltpu.VMEM((NX + 4, C, NY * NZ), bf16),
            pltpu.VMEM((2, C, NY * NZ), bf16),
            pltpu.VMEM((2, NX, C, NZ), bf16),
            pltpu.VMEM((4, C, NZ), bf16),
            pltpu.VMEM((K3, 7 * NZ), f32),
            pltpu.VMEM((2048, NZ), f32),
            pltpu.VMEM((GX, 256, NZ), f32),
            pltpu.VMEM((256, NZ), f32),
            pltpu.VMEM((GY, 16, NZ), f32),
            pltpu.VMEM((256, NZ), f32),
            pltpu.VMEM((2048, NZ), f32),
            dma((8,)), dma((8,)), dma((8,)), dma((8,)),
            dma((30,)), dma((30,)), dma((30,)), dma((30,)),
            dma((GX,)), dma((GX,)), dma((15,)), dma((15,)),
            dma((15,)), dma((15,)), dma((GX,)), dma((GX,)),
            dma((2,)),
        ],
        compiler_params=pltpu.CompilerParams(
            collective_id=0, has_side_effects=True, vmem_limit_bytes=60 * 1024 * 1024
        ),
    )(owners, features, active_mask, weight, channel_bias.reshape(1, C), cotangent)
    return pl.pallas_call(
        hand_over,
        out_shape=(
            jax.ShapeDtypeStruct((1, SLOTS, C, 512), bf16),
            jax.ShapeDtypeStruct((NX, NY, C, NZ), bf16),
            jax.ShapeDtypeStruct((3, 3, C, K3), f32),
        ),
        in_specs=[hbm, hbm, hbm],
        out_specs=(hbm, hbm, hbm),
        scratch_shapes=[dma((15,))],
    )(activations, grad_features, grad)


def solution(mesh):
    in_specs = (
        P("gx", "gy", None, None),
        P("gx", "gy", None),
        P("gx", "gy", None),
        P(),
        P(),
        P("gx", "gy", None, None),
    )
    out_specs = (P("gx", "gy", None, None), P("gx", "gy", None, None), P())
    return jax.shard_map(
        on_device, mesh=mesh, in_specs=in_specs, out_specs=out_specs, check_vma=False
    )
```

```python
import jax
import jax.numpy as jnp
from jax import lax
from jax.experimental import pallas as pl
from jax.experimental.pallas import tpu as pltpu
from jax.sharding import PartitionSpec as P

C = 96
NX = 8
NY = 8
NZ = 128
GX = 8
GY = 16
SLOTS = 32
K3 = 3 * C
K9 = 9 * C
TOTAL_SCALE = (NX * NY * NZ * GX * GY) ** -0.5
f32 = jnp.float32
bf16 = jnp.bfloat16
MESH = pl.DeviceIdType.MESH

PEERS = (
    (0, 1), (1, 0), (0, 3), (3, 0), (1, 1), (3, 3), (1, 3), (3, 1),
    (0, 2), (2, 0), (2, 1), (1, 2), (2, 3), (3, 2), (2, 2),
)
SIDES = ((1, 0), (-1, 0), (0, 1), (0, -1), (1, 1), (1, -1), (-1, 1), (-1, -1))


def swap_blocks(tiles):
    lane = lax.broadcasted_iota(jnp.int32, tiles[0].shape, 1)
    for step in (8, 4, 2, 1):
        width = step * 8
        upper = (lane // width) % 2 == 1
        moved = list(tiles)
        for i in range(16):
            if i & step:
                continue
            j = i | step
            low, high = tiles[i], tiles[j]
            moved[i] = jnp.where(upper, pltpu.roll(high, width, 1), low)
            moved[j] = jnp.where(upper, high, pltpu.roll(low, NZ - width, 1))
        tiles = moved
    return tiles


def put_stack(stack, x, y, tile, lane):
    zero = jnp.zeros_like(tile)
    stack[x, y, 0:C] = jnp.where(lane == 0, zero, pltpu.roll(tile, 1, 1))
    stack[x, y, C : 2 * C] = tile
    stack[x, y, 2 * C : K3] = jnp.where(lane == NZ - 1, zero, pltpu.roll(tile, NZ - 1, 1))


def conv_step(xi, kernel, stack, acc):
    rows = stack[xi].reshape((NY + 2) * K3, NZ)
    right = jnp.concatenate([rows[K3 * y : K3 * y + K9] for y in range(NY)], axis=1)
    product = jnp.dot(kernel[...], right, preferred_element_type=f32)
    acc[xi + 2] = product[0:C]
    acc[xi + 1] += product[C : 2 * C]
    acc[xi] += product[2 * C : K3]


def body(
    owners, feat, mask, weight, bias, cot_hbm,
    act_hbm, gf_out, gw_out,
    kernel_f, kernel_b, xp, xst, sst, acc, actz, bricks, send, recv, slz, hx, hy, hc, gwacc, red, r1, p1, r2, p3, fin,
    halo_send, halo_recv, shalo_send, shalo_recv, cot_send, cot_recv, act_send, act_recv,
    s1_send, s1_recv, s2_send, s2_recv, s3_send, s3_recv, s4_send, s4_recv, local_sem,
):
    gx = lax.axis_index("gx")
    gy = lax.axis_index("gy")
    gz = gy // 4
    gyy = gy % 4

    def ring_peer(n):
        dz, dy = PEERS[n]
        return ((gz + dz) % 4) * 4 + (gyy + dy) % 4

    def ring_source(n):
        dz, dy = PEERS[n]
        return ((gz + 4 - dz) % 4) * 4 + (gyy + 4 - dy) % 4

    def side(n, sign):
        dx, dy = SIDES[n]
        return ((gx + GX + sign * dx) % GX, (gy + GY + sign * dy) % GY)

    barrier = pltpu.get_barrier_semaphore()
    for n in range(15):
        pl.semaphore_signal(barrier, inc=1, device_id=(gx, ring_peer(n)), device_id_type=MESH)
    for d in range(1, GX):
        pl.semaphore_signal(barrier, inc=1, device_id=((gx + d) % GX, gy), device_id_type=MESH)
    for n in range(4, 8):
        pl.semaphore_signal(barrier, inc=1, device_id=side(n, 1), device_id_type=MESH)

    lane = lax.broadcasted_iota(jnp.int32, (C, NZ), 1)

    def mask_row(x, y):
        return jnp.broadcast_to(mask[x, pl.ds(y, 1)].astype(f32), (C, NZ))

    def masked(x, _):
        for y in range(NY):
            xp[x + 1, y + 1] = (feat[x, y].astype(f32) * mask_row(x, y)).astype(bf16)
        return 0

    lax.fori_loop(0, NX, masked, 0)
    pl.semaphore_wait(barrier, 26)

    def span(d, sign):
        if d == 0:
            return pl.ds(1, 8)
        if sign > 0:
            return 8 if d > 0 else 1
        return 0 if d > 0 else 9

    halos = []
    for n, (dx, dy) in enumerate(SIDES):
        halos.append(
            pltpu.make_async_remote_copy(
                src_ref=xp.at[span(dx, 1), span(dy, 1)],
                dst_ref=xp.at[span(dx, -1), span(dy, -1)],
                send_sem=halo_send.at[n],
                recv_sem=halo_recv.at[n],
                device_id=side(n, 1),
                device_id_type=MESH,
            )
        )
    for copy in halos:
        copy.start()

    def cot_copy(n, k):
        peer = ring_peer(n)
        return pltpu.make_async_remote_copy(
            src_ref=cot_hbm.at[0, 2 * peer + k],
            dst_ref=recv.at[2 * gy + k],
            send_sem=cot_send.at[15 * k + n],
            recv_sem=cot_recv.at[15 * k + n],
            device_id=(gx, peer),
            device_id_type=MESH,
        )

    cots = [cot_copy(n, k) for k in range(2) for n in range(15)]
    for copy in cots:
        copy.start()
    own_cot = pltpu.make_async_copy(
        cot_hbm.at[0, pl.ds(2 * gy, 2)], recv.at[pl.ds(2 * gy, 2)], local_sem.at[0]
    )
    own_cot.start()

    for a in range(3):
        kernel_f[C * a : C * a + C] = jnp.concatenate([weight[a, b] for b in range(3)], axis=1)
        blocks = []
        for b in range(3):
            turned = jnp.transpose(weight[2 - a, 2 - b].astype(f32))
            for c in range(3):
                blocks.append(turned[(2 - c) * C : (3 - c) * C].astype(bf16))
        kernel_b[C * a : C * a + C] = jnp.concatenate(blocks, axis=1)

    owner = [owners[0, 0, z] for z in range(16)]
    slots = []
    for z in range(16):
        rank = jnp.int32(0)
        for before in range(z):
            rank = rank + (owner[before] == owner[z]).astype(jnp.int32)
        slots.append(2 * owner[z] + rank)

    def stack_inner(x, _):
        for y in range(NY):
            put_stack(xst, x + 1, y + 1, xp[x + 1, y + 1], lane)
        return 0

    lax.fori_loop(0, NX, stack_inner, 0)
    for copy in halos:
        copy.wait()

    first_x = (gx > 0).astype(f32)
    last_x = (gx < GX - 1).astype(f32)
    first_y = (gy > 0).astype(f32)
    last_y = (gy < GY - 1).astype(f32)

    def keep(tile, flag):
        return (tile.astype(f32) * flag).astype(bf16)

    def stack_y(x, _):
        put_stack(xst, x, 0, keep(xp[x, 0], first_y), lane)
        put_stack(xst, x, 9, keep(xp[x, 9], last_y), lane)
        return 0

    lax.fori_loop(1, 9, stack_y, 0)

    def stack_x(y, _):
        put_stack(xst, 0, y, keep(xp[0, y], first_x), lane)
        put_stack(xst, 9, y, keep(xp[9, y], last_x), lane)
        return 0

    lax.fori_loop(1, 9, stack_x, 0)
    for x, y, flag in (
        (0, 0, first_x * first_y), (0, 9, first_x * last_y),
        (9, 0, last_x * first_y), (9, 9, last_x * last_y),
    ):
        put_stack(xst, x, y, keep(xp[x, y], flag), lane)

    acc[0] = jnp.zeros((C, NY * NZ), f32)
    acc[1] = jnp.zeros((C, NY * NZ), f32)

    def forward(xi, _):
        conv_step(xi, kernel_f, xst, acc)
        return 0

    lax.fori_loop(0, NX + 2, forward, 0)

    shift = jnp.transpose(jnp.broadcast_to(bias[...], (NZ, C)))

    def activate(x, _):
        for y in range(NY):
            cols = slice(NZ * y, NZ * y + NZ)
            pre = acc[x + 2, :, cols] + shift
            gate = jax.nn.sigmoid(pre)
            on = mask_row(x, y)
            actz[x, :, cols] = (on * pre * gate).astype(bf16)
            acc[x + 2, :, cols] = on * gate * (1.0 + pre * (1.0 - gate))
        return 0

    lax.fori_loop(0, NX, activate, 0)
    bricks[16] = jnp.zeros((C, 512), bf16)

    def to_bricks(n, _):
        u2 = n // 2
        rows = pl.ds(pl.multiple_of((n % 2) * 48, 48), 48)
        cols = pl.ds(pl.multiple_of(u2 * NZ, NZ), NZ)
        tiles = [actz[2 * u2 + j // 8, rows, (j % 8) * NZ : (j % 8) * NZ + NZ] for j in range(16)]
        for z, tile in enumerate(swap_blocks(tiles)):
            bricks[z, rows, cols] = tile
        return 0

    lax.fori_loop(0, 8, to_bricks, 0)

    def fill(s, _):
        brick = jnp.int32(16)
        for z in range(16):
            brick = jnp.where(slots[z] == s, z, brick)
        send[s] = bricks[brick]
        return 0

    lax.fori_loop(0, SLOTS, fill, 0)

    for n in range(2):
        slz[n] = jnp.zeros((C, NY * NZ), bf16)
        slz[10 + n] = jnp.zeros((C, NY * NZ), bf16)

    own_cot.wait()
    for copy in cots:
        copy.wait()

    def act_copy(n, k):
        peer = ring_peer(n)
        return pltpu.make_async_remote_copy(
            src_ref=send.at[2 * peer + k],
            dst_ref=act_hbm.at[0, 2 * gy + k],
            send_sem=act_send.at[15 * k + n],
            recv_sem=act_recv.at[15 * k + n],
            device_id=(gx, peer),
            device_id_type=MESH,
        )

    acts = [act_copy(n, k) for k in range(2) for n in range(15)]
    own_act = pltpu.make_async_copy(
        send.at[pl.ds(2 * gy, 2)], act_hbm.at[0, pl.ds(2 * gy, 2)], local_sem.at[1]
    )
    own_act.start()
    for copy in acts[:4]:
        copy.start()

    def to_slope(n, _):
        u2 = n // 2
        rows = pl.ds(pl.multiple_of((n % 2) * 48, 48), 48)
        cols = pl.ds(pl.multiple_of(u2 * NZ, NZ), NZ)
        tiles = [recv[slots[z], rows, cols] for z in range(16)]
        for j, tile in enumerate(swap_blocks(tiles)):
            part = slice((j % 8) * NZ, (j % 8) * NZ + NZ)
            row = 2 * u2 + j // 8 + 2
            slz[row, rows, part] = (tile.astype(f32) * acc[row, rows, part]).astype(bf16)
        return 0

    lax.fori_loop(0, 8, to_slope, 0)

    def edge(d):
        return 9 if d > 0 else 2

    def strip(d):
        return pl.ds(7 * NZ, NZ) if d > 0 else pl.ds(0, NZ)

    def low(d):
        return 0 if d > 0 else 1

    slope_halos = []
    for n, (dx, dy) in enumerate(SIDES):
        if dy == 0:
            source, target = slz.at[edge(dx)], hx.at[low(dx)]
        elif dx == 0:
            source, target = slz.at[pl.ds(2, 8), :, strip(dy)], hy.at[low(dy)]
        else:
            source, target = slz.at[edge(dx), :, strip(dy)], hc.at[2 * low(dx) + low(dy)]
        slope_halos.append(
            pltpu.make_async_remote_copy(
                src_ref=source,
                dst_ref=target,
                send_sem=shalo_send.at[n],
                recv_sem=shalo_recv.at[n],
                device_id=side(n, 1),
                device_id_type=MESH,
            )
        )
    for copy in slope_halos:
        copy.start()
    for copy in acts[4:15]:
        copy.start()

    gwacc[...] = jnp.zeros((K3, 7 * NZ), f32)

    def weight_terms(xi, _):
        left = jnp.concatenate([slz[xi + 2], slz[xi + 1], slz[xi]], axis=0)
        rows = xst[xi].reshape((NY + 2) * K3, NZ)
        right = jnp.concatenate([rows[K3 * y : K3 * y + K9] for y in range(NY)], axis=1)
        gwacc[:, 0:K9] += lax.dot_general(
            left, right, (((1,), (1,)), ((), ())), preferred_element_type=f32
        )
        return 0

    lax.fori_loop(0, NX + 2, weight_terms, 0)
    for j in range(7):
        red[K3 * j : K3 * j + K3] = gwacc[:, NZ * j : NZ * j + NZ]
    red[7 * K3 : 2048] = jnp.zeros((2048 - 7 * K3, NZ), f32)

    def stage1(d):
        peer = (gx + d) % GX
        return pltpu.make_async_remote_copy(
            src_ref=red.at[pl.ds(256 * peer, 256)],
            dst_ref=r1.at[gx],
            send_sem=s1_send.at[d],
            recv_sem=s1_recv.at[d],
            device_id=(peer, gy),
            device_id_type=MESH,
        )

    ones = [stage1(d) for d in range(1, GX)]
    for copy in ones:
        copy.start()

    def slope_inner(x, _):
        for y in range(NY):
            put_stack(sst, x + 1, y + 1, slz[x + 2, :, NZ * y : NZ * y + NZ], lane)
        return 0

    lax.fori_loop(0, NX, slope_inner, 0)
    for copy in slope_halos:
        copy.wait()

    def slope_y(x, _):
        put_stack(sst, x + 1, 0, keep(hy[0, x], first_y), lane)
        put_stack(sst, x + 1, 9, keep(hy[1, x], last_y), lane)
        return 0

    lax.fori_loop(0, NX, slope_y, 0)
    for y in range(NY):
        cols = slice(NZ * y, NZ * y + NZ)
        put_stack(sst, 0, y + 1, keep(hx[0, :, cols], first_x), lane)
        put_stack(sst, 9, y + 1, keep(hx[1, :, cols], last_x), lane)
    for n, x, y, flag in (
        (0, 0, 0, first_x * first_y), (1, 0, 9, first_x * last_y),
        (2, 9, 0, last_x * first_y), (3, 9, 9, last_x * last_y),
    ):
        put_stack(sst, x, y, keep(hc[n], flag), lane)

    for copy in ones:
        copy.wait()
    total = red[pl.ds(pl.multiple_of(256 * gx, 256), 256)]
    for d in range(1, GX):
        total = total + r1[(gx + GX - d) % GX]
    p1[...] = total

    def stage2(n):
        peer = ring_peer(n)
        return pltpu.make_async_remote_copy(
            src_ref=p1.at[pl.ds(16 * peer, 16)],
            dst_ref=r2.at[gy],
            send_sem=s2_send.at[n],
            recv_sem=s2_recv.at[n],
            device_id=(gx, peer),
            device_id_type=MESH,
        )

    twos = [stage2(n) for n in range(15)]
    for copy in twos:
        copy.start()
    for copy in acts[15:18]:
        copy.start()

    def backward(xi, _):
        conv_step(xi, kernel_b, sst, acc)
        return 0

    lax.fori_loop(0, 4, backward, 0)

    for copy in twos:
        copy.wait()
    part = p1[pl.ds(pl.multiple_of(16 * gy, 16), 16)]
    for n in range(15):
        part = part + r2[ring_source(n)]
    mine = pl.ds(pl.multiple_of(16 * gy, 16), 16)
    p3[mine] = part * TOTAL_SCALE

    def stage3(n):
        return pltpu.make_async_remote_copy(
            src_ref=p3.at[mine],
            dst_ref=p3.at[mine],
            send_sem=s3_send.at[n],
            recv_sem=s3_recv.at[n],
            device_id=(gx, ring_peer(n)),
            device_id_type=MESH,
        )

    threes = [stage3(n) for n in range(15)]
    for copy in threes:
        copy.start()
    for copy in acts[18:]:
        copy.start()
    lax.fori_loop(4, 7, backward, 0)
    for copy in threes:
        copy.wait()

    block = pl.ds(pl.multiple_of(256 * gx, 256), 256)

    def stage4(d):
        return pltpu.make_async_remote_copy(
            src_ref=p3,
            dst_ref=fin.at[block],
            send_sem=s4_send.at[d],
            recv_sem=s4_recv.at[d],
            device_id=((gx + d) % GX, gy),
            device_id_type=MESH,
        )

    fours = [stage4(d) for d in range(1, GX)]
    for copy in fours:
        copy.start()
    fin[block] = p3[...]
    lax.fori_loop(7, NX + 2, backward, 0)

    def finish(x, _):
        for y in range(NY):
            gf_out[x, y] = (mask_row(x, y) * acc[x + 2, :, NZ * y : NZ * y + NZ]).astype(bf16)
        return 0

    lax.fori_loop(0, NX, finish, 0)
    for copy in fours:
        copy.wait()
    full = jnp.concatenate([fin[K3 * j : K3 * j + K3] for j in range(7)], axis=1)
    for a in range(3):
        for b in range(3):
            gw_out[a, b] = full[C * a : C * a + C, K3 * b : K3 * b + K3]
    own_act.wait()
    for copy in acts:
        copy.wait()


def hand_over(act, gf, gw, act_out, gf_out, gw_out, act_v, gf_v, gw_v, read_sems, write_sems):
    pieces = [(act, act_v, act_out, (0, pl.ds(4 * n, 4))) for n in range(8)]
    pieces += [(gf, gf_v, gf_out, (pl.ds(2 * n, 2),)) for n in range(4)]
    pieces += [(gw, gw_v, gw_out, (n,)) for n in range(3)]
    reads = [
        pltpu.make_async_copy(source.at[part], stage.at[part], read_sems.at[n])
        for n, (source, stage, _, part) in enumerate(pieces)
    ]
    writes = [
        pltpu.make_async_copy(stage.at[part], target.at[part], write_sems.at[n])
        for n, (_, stage, target, part) in enumerate(pieces)
    ]
    for copy in reads:
        copy.start()
    for read, write in zip(reads, writes):
        read.wait()
        write.start()
    for copy in writes:
        copy.wait()


def on_device(features, active_mask, owners, weight, channel_bias, cotangent):
    smem = pl.BlockSpec(memory_space=pltpu.SMEM)
    vmem = pl.BlockSpec(memory_space=pltpu.VMEM)
    hbm = pl.BlockSpec(memory_space=pl.ANY)
    dma = pltpu.SemaphoreType.DMA
    activations, grad_features, grad = pl.pallas_call(
        body,
        out_shape=(
            jax.ShapeDtypeStruct((1, SLOTS, C, 512), bf16),
            jax.ShapeDtypeStruct((NX, NY, C, NZ), bf16),
            jax.ShapeDtypeStruct((3, 3, C, K3), f32),
        ),
        in_specs=[smem, vmem, vmem, vmem, vmem, hbm],
        out_specs=(hbm, vmem, vmem),
        scratch_shapes=[
            pltpu.VMEM((K3, K9), bf16),
            pltpu.VMEM((K3, K9), bf16),
            pltpu.VMEM((NX + 2, NY + 2, C, NZ), bf16),
            pltpu.VMEM((NX + 2, NY + 2, K3, NZ), bf16),
            pltpu.VMEM((NX + 2, NY + 2, K3, NZ), bf16),
            pltpu.VMEM((NX + 4, C, NY * NZ), f32),
            pltpu.VMEM((NX, C, NY * NZ), bf16),
            pltpu.VMEM((17, C, 512), bf16),
            pltpu.VMEM((SLOTS, C, 512), bf16),
            pltpu.VMEM((SLOTS, C, 512), bf16),
            pltpu.VMEM((NX + 4, C, NY * NZ), bf16),
            pltpu.VMEM((2, C, NY * NZ), bf16),
            pltpu.VMEM((2, NX, C, NZ), bf16),
            pltpu.VMEM((4, C, NZ), bf16),
            pltpu.VMEM((K3, 7 * NZ), f32),
            pltpu.VMEM((2048, NZ), f32),
            pltpu.VMEM((GX, 256, NZ), f32),
            pltpu.VMEM((256, NZ), f32),
            pltpu.VMEM((GY, 16, NZ), f32),
            pltpu.VMEM((256, NZ), f32),
            pltpu.VMEM((2048, NZ), f32),
            dma((8,)), dma((8,)), dma((8,)), dma((8,)),
            dma((30,)), dma((30,)), dma((30,)), dma((30,)),
            dma((GX,)), dma((GX,)), dma((15,)), dma((15,)),
            dma((15,)), dma((15,)), dma((GX,)), dma((GX,)),
            dma((2,)),
        ],
        compiler_params=pltpu.CompilerParams(
            collective_id=0, has_side_effects=True, vmem_limit_bytes=60 * 1024 * 1024
        ),
    )(owners, features, active_mask, weight, channel_bias.reshape(1, C), cotangent)
    return pl.pallas_call(
        hand_over,
        out_shape=(
            jax.ShapeDtypeStruct((1, SLOTS, C, 512), bf16),
            jax.ShapeDtypeStruct((NX, NY, C, NZ), bf16),
            jax.ShapeDtypeStruct((3, 3, C, K3), f32),
        ),
        in_specs=[hbm, hbm, hbm],
        out_specs=(hbm, hbm, hbm),
        scratch_shapes=[
            pltpu.VMEM((1, SLOTS, C, 512), bf16),
            pltpu.VMEM((NX, NY, C, NZ), bf16),
            pltpu.VMEM((3, 3, C, K3), f32),
            dma((15,)),
            dma((15,)),
        ],
    )(activations, grad_features, grad)


def solution(mesh):
    in_specs = (
        P("gx", "gy", None, None),
        P("gx", "gy", None),
        P("gx", "gy", None),
        P(),
        P(),
        P("gx", "gy", None, None),
    )
    out_specs = (P("gx", "gy", None, None), P("gx", "gy", None, None), P())
    return jax.shard_map(
        on_device, mesh=mesh, in_specs=in_specs, out_specs=out_specs, check_vma=False
    )
```

```python
import jax
import jax.numpy as jnp
from jax import lax
from jax.experimental import pallas as pl
from jax.experimental.pallas import tpu as pltpu
from jax.sharding import PartitionSpec as P

C = 96
NX = 8
NY = 8
NZ = 128
GX = 8
GY = 16
SLOTS = 32
K3 = 3 * C
K9 = 9 * C
TOTAL_SCALE = (NX * NY * NZ * GX * GY) ** -0.5
f32 = jnp.float32
bf16 = jnp.bfloat16
MESH = pl.DeviceIdType.MESH

PEERS = (
    (0, 1), (1, 0), (0, 3), (3, 0), (1, 1), (3, 3), (1, 3), (3, 1),
    (0, 2), (2, 0), (2, 1), (1, 2), (2, 3), (3, 2), (2, 2),
)
SIDES = ((1, 0), (-1, 0), (0, 1), (0, -1), (1, 1), (1, -1), (-1, 1), (-1, -1))


def swap_blocks(tiles):
    lane = lax.broadcasted_iota(jnp.int32, tiles[0].shape, 1)
    for step in (8, 4, 2, 1):
        width = step * 8
        upper = (lane // width) % 2 == 1
        moved = list(tiles)
        for i in range(16):
            if i & step:
                continue
            j = i | step
            low, high = tiles[i], tiles[j]
            moved[i] = jnp.where(upper, pltpu.roll(high, width, 1), low)
            moved[j] = jnp.where(upper, high, pltpu.roll(low, NZ - width, 1))
        tiles = moved
    return tiles


def put_stack(stack, x, y, tile, lane):
    zero = jnp.zeros_like(tile)
    stack[x, y, 0:C] = jnp.where(lane == 0, zero, pltpu.roll(tile, 1, 1))
    stack[x, y, C : 2 * C] = tile
    stack[x, y, 2 * C : K3] = jnp.where(lane == NZ - 1, zero, pltpu.roll(tile, NZ - 1, 1))


def conv_step(xi, kernel, stack, acc):
    rows = stack[xi].reshape((NY + 2) * K3, NZ)
    right = jnp.concatenate([rows[K3 * y : K3 * y + K9] for y in range(NY)], axis=1)
    product = jnp.dot(kernel[...], right, preferred_element_type=f32)
    acc[xi + 2] = product[0:C]
    acc[xi + 1] += product[C : 2 * C]
    acc[xi] += product[2 * C : K3]


def body(
    owners, feat, mask, weight, bias, cot_hbm,
    act_hbm, gf_out, gw_out,
    kernel_f, kernel_b, xp, xst, sst, acc, actz, bricks, send, recv, slz, hx, hy, hc, gwacc, red, rp, p0, r1, p1, r2, p3, fin,
    halo_send, halo_recv, shalo_send, shalo_recv, cot_send, cot_recv, act_send, act_recv,
    s1_send, s1_recv, s2_send, s2_recv, s3_send, s3_recv, s4_send, s4_recv, pair_sem, local_sem,
):
    gx = lax.axis_index("gx")
    gy = lax.axis_index("gy")
    gz = gy // 4
    gyy = gy % 4

    def ring_peer(n):
        dz, dy = PEERS[n]
        return ((gz + dz) % 4) * 4 + (gyy + dy) % 4

    def ring_source(n):
        dz, dy = PEERS[n]
        return ((gz + 4 - dz) % 4) * 4 + (gyy + 4 - dy) % 4

    def side(n, sign):
        dx, dy = SIDES[n]
        return ((gx + GX + sign * dx) % GX, (gy + GY + sign * dy) % GY)

    barrier = pltpu.get_barrier_semaphore()
    for n in range(15):
        pl.semaphore_signal(barrier, inc=1, device_id=(gx, ring_peer(n)), device_id_type=MESH)
    for d in range(1, GX):
        pl.semaphore_signal(barrier, inc=1, device_id=((gx + d) % GX, gy), device_id_type=MESH)
    for n in range(4, 8):
        pl.semaphore_signal(barrier, inc=1, device_id=side(n, 1), device_id_type=MESH)

    lane = lax.broadcasted_iota(jnp.int32, (C, NZ), 1)

    def mask_row(x, y):
        return jnp.broadcast_to(mask[x, pl.ds(y, 1)].astype(f32), (C, NZ))

    def masked(x, _):
        for y in range(NY):
            xp[x + 1, y + 1] = (feat[x, y].astype(f32) * mask_row(x, y)).astype(bf16)
        return 0

    lax.fori_loop(0, NX, masked, 0)
    pl.semaphore_wait(barrier, 26)

    def span(d, sign):
        if d == 0:
            return pl.ds(1, 8)
        if sign > 0:
            return 8 if d > 0 else 1
        return 0 if d > 0 else 9

    halos = []
    for n, (dx, dy) in enumerate(SIDES):
        halos.append(
            pltpu.make_async_remote_copy(
                src_ref=xp.at[span(dx, 1), span(dy, 1)],
                dst_ref=xp.at[span(dx, -1), span(dy, -1)],
                send_sem=halo_send.at[n],
                recv_sem=halo_recv.at[n],
                device_id=side(n, 1),
                device_id_type=MESH,
            )
        )
    for copy in halos:
        copy.start()

    def cot_copy(n, k):
        peer = ring_peer(n)
        return pltpu.make_async_remote_copy(
            src_ref=cot_hbm.at[0, 2 * peer + k],
            dst_ref=recv.at[2 * gy + k],
            send_sem=cot_send.at[15 * k + n],
            recv_sem=cot_recv.at[15 * k + n],
            device_id=(gx, peer),
            device_id_type=MESH,
        )

    cots = [cot_copy(n, k) for k in range(2) for n in range(15)]
    for copy in cots:
        copy.start()
    own_cot = pltpu.make_async_copy(
        cot_hbm.at[0, pl.ds(2 * gy, 2)], recv.at[pl.ds(2 * gy, 2)], local_sem.at[0]
    )
    own_cot.start()

    for a in range(3):
        kernel_f[C * a : C * a + C] = jnp.concatenate([weight[a, b] for b in range(3)], axis=1)
        blocks = []
        for b in range(3):
            turned = jnp.transpose(weight[2 - a, 2 - b].astype(f32))
            for c in range(3):
                blocks.append(turned[(2 - c) * C : (3 - c) * C].astype(bf16))
        kernel_b[C * a : C * a + C] = jnp.concatenate(blocks, axis=1)

    owner = [owners[0, 0, z] for z in range(16)]
    slots = []
    for z in range(16):
        rank = jnp.int32(0)
        for before in range(z):
            rank = rank + (owner[before] == owner[z]).astype(jnp.int32)
        slots.append(2 * owner[z] + rank)

    def stack_inner(x, _):
        for y in range(NY):
            put_stack(xst, x + 1, y + 1, xp[x + 1, y + 1], lane)
        return 0

    lax.fori_loop(0, NX, stack_inner, 0)
    for copy in halos:
        copy.wait()

    first_x = (gx > 0).astype(f32)
    last_x = (gx < GX - 1).astype(f32)
    first_y = (gy > 0).astype(f32)
    last_y = (gy < GY - 1).astype(f32)

    def keep(tile, flag):
        return (tile.astype(f32) * flag).astype(bf16)

    def stack_y(x, _):
        put_stack(xst, x, 0, keep(xp[x, 0], first_y), lane)
        put_stack(xst, x, 9, keep(xp[x, 9], last_y), lane)
        return 0

    lax.fori_loop(1, 9, stack_y, 0)

    def stack_x(y, _):
        put_stack(xst, 0, y, keep(xp[0, y], first_x), lane)
        put_stack(xst, 9, y, keep(xp[9, y], last_x), lane)
        return 0

    lax.fori_loop(1, 9, stack_x, 0)
    for x, y, flag in (
        (0, 0, first_x * first_y), (0, 9, first_x * last_y),
        (9, 0, last_x * first_y), (9, 9, last_x * last_y),
    ):
        put_stack(xst, x, y, keep(xp[x, y], flag), lane)

    acc[0] = jnp.zeros((C, NY * NZ), f32)
    acc[1] = jnp.zeros((C, NY * NZ), f32)

    def forward(xi, _):
        conv_step(xi, kernel_f, xst, acc)
        return 0

    lax.fori_loop(0, NX + 2, forward, 0)

    shift = jnp.transpose(jnp.broadcast_to(bias[...], (NZ, C)))

    def activate(x, _):
        for y in range(NY):
            cols = slice(NZ * y, NZ * y + NZ)
            pre = acc[x + 2, :, cols] + shift
            gate = jax.nn.sigmoid(pre)
            on = mask_row(x, y)
            actz[x, :, cols] = (on * pre * gate).astype(bf16)
            acc[x + 2, :, cols] = on * gate * (1.0 + pre * (1.0 - gate))
        return 0

    lax.fori_loop(0, NX, activate, 0)
    bricks[16] = jnp.zeros((C, 512), bf16)

    def to_bricks(n, _):
        u2 = n // 2
        rows = pl.ds(pl.multiple_of((n % 2) * 48, 48), 48)
        cols = pl.ds(pl.multiple_of(u2 * NZ, NZ), NZ)
        tiles = [actz[2 * u2 + j // 8, rows, (j % 8) * NZ : (j % 8) * NZ + NZ] for j in range(16)]
        for z, tile in enumerate(swap_blocks(tiles)):
            bricks[z, rows, cols] = tile
        return 0

    lax.fori_loop(0, 8, to_bricks, 0)

    def fill(s, _):
        brick = jnp.int32(16)
        for z in range(16):
            brick = jnp.where(slots[z] == s, z, brick)
        send[s] = bricks[brick]
        return 0

    lax.fori_loop(0, SLOTS, fill, 0)

    for n in range(2):
        slz[n] = jnp.zeros((C, NY * NZ), bf16)
        slz[10 + n] = jnp.zeros((C, NY * NZ), bf16)

    own_cot.wait()
    for copy in cots:
        copy.wait()

    def act_copy(n, k):
        peer = ring_peer(n)
        return pltpu.make_async_remote_copy(
            src_ref=send.at[2 * peer + k],
            dst_ref=act_hbm.at[0, 2 * gy + k],
            send_sem=act_send.at[15 * k + n],
            recv_sem=act_recv.at[15 * k + n],
            device_id=(gx, peer),
            device_id_type=MESH,
        )

    acts = [act_copy(n, k) for k in range(2) for n in range(15)]
    own_act = pltpu.make_async_copy(
        send.at[pl.ds(2 * gy, 2)], act_hbm.at[0, pl.ds(2 * gy, 2)], local_sem.at[1]
    )
    own_act.start()
    for copy in acts[:8]:
        copy.start()

    def to_slope(n, _):
        u2 = n // 2
        rows = pl.ds(pl.multiple_of((n % 2) * 48, 48), 48)
        cols = pl.ds(pl.multiple_of(u2 * NZ, NZ), NZ)
        tiles = [recv[slots[z], rows, cols] for z in range(16)]
        for j, tile in enumerate(swap_blocks(tiles)):
            part = slice((j % 8) * NZ, (j % 8) * NZ + NZ)
            row = 2 * u2 + j // 8 + 2
            slz[row, rows, part] = (tile.astype(f32) * acc[row, rows, part]).astype(bf16)
        return 0

    lax.fori_loop(0, 8, to_slope, 0)

    def edge(d):
        return 9 if d > 0 else 2

    def strip(d):
        return pl.ds(7 * NZ, NZ) if d > 0 else pl.ds(0, NZ)

    def low(d):
        return 0 if d > 0 else 1

    slope_halos = []
    for n, (dx, dy) in enumerate(SIDES):
        if dy == 0:
            source, target = slz.at[edge(dx)], hx.at[low(dx)]
        elif dx == 0:
            source, target = slz.at[pl.ds(2, 8), :, strip(dy)], hy.at[low(dy)]
        else:
            source, target = slz.at[edge(dx), :, strip(dy)], hc.at[2 * low(dx) + low(dy)]
        slope_halos.append(
            pltpu.make_async_remote_copy(
                src_ref=source,
                dst_ref=target,
                send_sem=shalo_send.at[n],
                recv_sem=shalo_recv.at[n],
                device_id=side(n, 1),
                device_id_type=MESH,
            )
        )
    for copy in slope_halos:
        copy.start()
    for copy in acts[8:10]:
        copy.start()

    gwacc[...] = jnp.zeros((K3, 7 * NZ), f32)

    def weight_terms(xi, _):
        left = jnp.concatenate([slz[xi + 2], slz[xi + 1], slz[xi]], axis=0)
        rows = xst[xi].reshape((NY + 2) * K3, NZ)
        right = jnp.concatenate([rows[K3 * y : K3 * y + K9] for y in range(NY)], axis=1)
        gwacc[:, 0:K9] += lax.dot_general(
            left, right, (((1,), (1,)), ((), ())), preferred_element_type=f32
        )
        return 0

    lax.fori_loop(0, 5, weight_terms, 0)
    for copy in acts[10:14]:
        copy.start()
    lax.fori_loop(5, NX + 2, weight_terms, 0)
    for j in range(7):
        red[K3 * j : K3 * j + K3] = gwacc[:, NZ * j : NZ * j + NZ]
    red[7 * K3 : 2048] = jnp.zeros((2048 - 7 * K3, NZ), f32)

    cx = gx // 2
    core = gx % 2
    partner = cx * 2 + 1 - core
    half = pl.ds(pl.multiple_of(1024 * core, 1024), 1024)

    def chip(d):
        return ((cx + d) % 4) * 2 + core

    pair = pltpu.make_async_remote_copy(
        src_ref=red.at[pl.ds(1024 * (1 - core), 1024)],
        dst_ref=rp,
        send_sem=pair_sem.at[0],
        recv_sem=pair_sem.at[1],
        device_id=(partner, gy),
        device_id_type=MESH,
    )
    pair.start()
    for copy in acts[14:16]:
        copy.start()

    def slope_inner(x, _):
        for y in range(NY):
            put_stack(sst, x + 1, y + 1, slz[x + 2, :, NZ * y : NZ * y + NZ], lane)
        return 0

    lax.fori_loop(0, NX, slope_inner, 0)
    pair.wait()
    p0[...] = red[half] + rp[...]

    def stage1(d):
        return pltpu.make_async_remote_copy(
            src_ref=p0.at[pl.ds(256 * ((cx + d) % 4), 256)],
            dst_ref=r1.at[d - 1],
            send_sem=s1_send.at[d],
            recv_sem=s1_recv.at[d],
            device_id=(chip(d), gy),
            device_id_type=MESH,
        )

    ones = [stage1(d) for d in range(1, 4)]
    for copy in ones:
        copy.start()
    for copy in acts[16:18]:
        copy.start()
    for copy in slope_halos:
        copy.wait()

    def slope_y(x, _):
        put_stack(sst, x + 1, 0, keep(hy[0, x], first_y), lane)
        put_stack(sst, x + 1, 9, keep(hy[1, x], last_y), lane)
        return 0

    lax.fori_loop(0, NX, slope_y, 0)
    for y in range(NY):
        cols = slice(NZ * y, NZ * y + NZ)
        put_stack(sst, 0, y + 1, keep(hx[0, :, cols], first_x), lane)
        put_stack(sst, 9, y + 1, keep(hx[1, :, cols], last_x), lane)
    for n, x, y, flag in (
        (0, 0, 0, first_x * first_y), (1, 0, 9, first_x * last_y),
        (2, 9, 0, last_x * first_y), (3, 9, 9, last_x * last_y),
    ):
        put_stack(sst, x, y, keep(hc[n], flag), lane)

    def backward(xi, _):
        conv_step(xi, kernel_b, sst, acc)
        return 0

    lax.fori_loop(0, 3, backward, 0)

    for copy in ones:
        copy.wait()
    p1[...] = p0[pl.ds(pl.multiple_of(256 * cx, 256), 256)] + r1[0] + r1[1] + r1[2]

    def stage2(n):
        peer = ring_peer(n)
        return pltpu.make_async_remote_copy(
            src_ref=p1.at[pl.ds(16 * peer, 16)],
            dst_ref=r2.at[gy],
            send_sem=s2_send.at[n],
            recv_sem=s2_recv.at[n],
            device_id=(gx, peer),
            device_id_type=MESH,
        )

    twos = [stage2(n) for n in range(15)]
    for copy in twos:
        copy.start()
    for copy in acts[18:20]:
        copy.start()
    lax.fori_loop(3, 6, backward, 0)
    for copy in twos:
        copy.wait()
    part = p1[pl.ds(pl.multiple_of(16 * gy, 16), 16)]
    for n in range(15):
        part = part + r2[ring_source(n)]
    mine = pl.ds(pl.multiple_of(16 * gy, 16), 16)
    p3[mine] = part * TOTAL_SCALE

    def stage3(n):
        return pltpu.make_async_remote_copy(
            src_ref=p3.at[mine],
            dst_ref=p3.at[mine],
            send_sem=s3_send.at[n],
            recv_sem=s3_recv.at[n],
            device_id=(gx, ring_peer(n)),
            device_id_type=MESH,
        )

    threes = [stage3(n) for n in range(15)]
    for copy in threes:
        copy.start()
    for copy in acts[20:23]:
        copy.start()
    lax.fori_loop(6, 8, backward, 0)
    for copy in threes:
        copy.wait()

    block = pl.ds(pl.multiple_of(1024 * core + 256 * cx, 256), 256)

    def stage4(d):
        return pltpu.make_async_remote_copy(
            src_ref=p3,
            dst_ref=fin.at[block],
            send_sem=s4_send.at[d],
            recv_sem=s4_recv.at[d],
            device_id=(chip(d), gy),
            device_id_type=MESH,
        )

    fours = [stage4(d) for d in range(1, 4)]
    for copy in fours:
        copy.start()
    for copy in acts[23:]:
        copy.start()
    fin[block] = p3[...]
    lax.fori_loop(8, NX + 2, backward, 0)

    def finish(x, _):
        for y in range(NY):
            gf_out[x, y] = (mask_row(x, y) * acc[x + 2, :, NZ * y : NZ * y + NZ]).astype(bf16)
        return 0

    lax.fori_loop(0, NX, finish, 0)
    for copy in fours:
        copy.wait()
    back = pltpu.make_async_remote_copy(
        src_ref=fin.at[half],
        dst_ref=fin.at[half],
        send_sem=pair_sem.at[2],
        recv_sem=pair_sem.at[3],
        device_id=(partner, gy),
        device_id_type=MESH,
    )
    back.start()
    back.wait()
    full = jnp.concatenate([fin[K3 * j : K3 * j + K3] for j in range(7)], axis=1)
    for a in range(3):
        for b in range(3):
            gw_out[a, b] = full[C * a : C * a + C, K3 * b : K3 * b + K3]
    own_act.wait()
    for copy in acts:
        copy.wait()


def hand_over(act, gf, gw, act_out, gf_out, gw_out, sems):
    pieces = [(act, act_out, (0, pl.ds(4 * n, 4))) for n in range(8)]
    pieces += [(gf, gf_out, (pl.ds(2 * n, 2),)) for n in range(4)]
    pieces += [(gw, gw_out, (n,)) for n in range(3)]
    copies = [
        pltpu.make_async_copy(source.at[part], target.at[part], sems.at[n])
        for n, (source, target, part) in enumerate(pieces)
    ]
    for copy in copies:
        copy.start()
    for copy in copies:
        copy.wait()


def on_device(features, active_mask, owners, weight, channel_bias, cotangent):
    smem = pl.BlockSpec(memory_space=pltpu.SMEM)
    vmem = pl.BlockSpec(memory_space=pltpu.VMEM)
    hbm = pl.BlockSpec(memory_space=pl.ANY)
    dma = pltpu.SemaphoreType.DMA
    activations, grad_features, grad = pl.pallas_call(
        body,
        out_shape=(
            pltpu.VMEM((1, SLOTS, C, 512), bf16),
            pltpu.VMEM((NX, NY, C, NZ), bf16),
            pltpu.VMEM((3, 3, C, K3), f32),
        ),
        in_specs=[smem, vmem, vmem, vmem, vmem, hbm],
        out_specs=(vmem, vmem, vmem),
        scratch_shapes=[
            pltpu.VMEM((K3, K9), bf16),
            pltpu.VMEM((K3, K9), bf16),
            pltpu.VMEM((NX + 2, NY + 2, C, NZ), bf16),
            pltpu.VMEM((NX + 2, NY + 2, K3, NZ), bf16),
            pltpu.VMEM((NX + 2, NY + 2, K3, NZ), bf16),
            pltpu.VMEM((NX + 4, C, NY * NZ), f32),
            pltpu.VMEM((NX, C, NY * NZ), bf16),
            pltpu.VMEM((17, C, 512), bf16),
            pltpu.VMEM((SLOTS, C, 512), bf16),
            pltpu.VMEM((SLOTS, C, 512), bf16),
            pltpu.VMEM((NX + 4, C, NY * NZ), bf16),
            pltpu.VMEM((2, C, NY * NZ), bf16),
            pltpu.VMEM((2, NX, C, NZ), bf16),
            pltpu.VMEM((4, C, NZ), bf16),
            pltpu.VMEM((K3, 7 * NZ), f32),
            pltpu.VMEM((2048, NZ), f32),
            pltpu.VMEM((1024, NZ), f32),
            pltpu.VMEM((1024, NZ), f32),
            pltpu.VMEM((3, 256, NZ), f32),
            pltpu.VMEM((256, NZ), f32),
            pltpu.VMEM((GY, 16, NZ), f32),
            pltpu.VMEM((256, NZ), f32),
            pltpu.VMEM((2048, NZ), f32),
            dma((8,)), dma((8,)), dma((8,)), dma((8,)),
            dma((30,)), dma((30,)), dma((30,)), dma((30,)),
            dma((4,)), dma((4,)), dma((15,)), dma((15,)),
            dma((15,)), dma((15,)), dma((4,)), dma((4,)),
            dma((4,)), dma((2,)),
        ],
        compiler_params=pltpu.CompilerParams(
            collective_id=0, has_side_effects=True, vmem_limit_bytes=52 * 1024 * 1024
        ),
    )(owners, features, active_mask, weight, channel_bias.reshape(1, C), cotangent)
    return pl.pallas_call(
        hand_over,
        out_shape=(
            jax.ShapeDtypeStruct((1, SLOTS, C, 512), bf16),
            jax.ShapeDtypeStruct((NX, NY, C, NZ), bf16),
            jax.ShapeDtypeStruct((3, 3, C, K3), f32),
        ),
        in_specs=[vmem, vmem, vmem],
        out_specs=(hbm, hbm, hbm),
        scratch_shapes=[
            dma((15,)),
        ],
        compiler_params=pltpu.CompilerParams(vmem_limit_bytes=1024 * 1024),
    )(*(pltpu.with_memory_space_constraint(r, pltpu.VMEM) for r in (activations, grad_features, grad)))


def solution(mesh):
    in_specs = (
        P("gx", "gy", None, None),
        P("gx", "gy", None),
        P("gx", "gy", None),
        P(),
        P(),
        P("gx", "gy", None, None),
    )
    out_specs = (P("gx", "gy", None, None), P("gx", "gy", None, None), P())
    return jax.shard_map(
        on_device, mesh=mesh, in_specs=in_specs, out_specs=out_specs, check_vma=False
    )
```

```python
import jax
import jax.numpy as jnp
from jax import lax
from jax.experimental import pallas as pl
from jax.experimental.pallas import tpu as pltpu
from jax.sharding import PartitionSpec as P

C = 96
NX = 8
NY = 8
NZ = 128
GX = 8
GY = 16
SLOTS = 32
K3 = 3 * C
K9 = 9 * C
TOTAL_SCALE = (NX * NY * NZ * GX * GY) ** -0.5
f32 = jnp.float32
bf16 = jnp.bfloat16
MESH = pl.DeviceIdType.MESH

PEERS = (
    (0, 1), (1, 0), (0, 3), (3, 0), (1, 1), (3, 3), (1, 3), (3, 1),
    (0, 2), (2, 0), (2, 1), (1, 2), (2, 3), (3, 2), (2, 2),
)
SIDES = ((1, 0), (-1, 0), (0, 1), (0, -1), (1, 1), (1, -1), (-1, 1), (-1, -1))


def swap_blocks(tiles):
    lane = lax.broadcasted_iota(jnp.int32, tiles[0].shape, 1)
    for step in (8, 4, 2, 1):
        width = step * 8
        upper = (lane // width) % 2 == 1
        moved = list(tiles)
        for i in range(16):
            if i & step:
                continue
            j = i | step
            low, high = tiles[i], tiles[j]
            moved[i] = jnp.where(upper, pltpu.roll(high, width, 1), low)
            moved[j] = jnp.where(upper, high, pltpu.roll(low, NZ - width, 1))
        tiles = moved
    return tiles


def put_stack(stack, x, y, tile, lane):
    zero = jnp.zeros_like(tile)
    stack[x, y, 0:C] = jnp.where(lane == 0, zero, pltpu.roll(tile, 1, 1))
    stack[x, y, C : 2 * C] = tile
    stack[x, y, 2 * C : K3] = jnp.where(lane == NZ - 1, zero, pltpu.roll(tile, NZ - 1, 1))


def conv_step(xi, kernel, stack, acc):
    rows = stack[xi].reshape((NY + 2) * K3, NZ)
    right = jnp.concatenate([rows[K3 * y : K3 * y + K9] for y in range(NY)], axis=1)
    product = jnp.dot(kernel[...], right, preferred_element_type=f32)
    acc[xi + 2] = product[0:C]
    acc[xi + 1] += product[C : 2 * C]
    acc[xi] += product[2 * C : K3]


def body(
    owners, feat, mask, weight, bias, cot_hbm,
    act_hbm, gf_out, gw_out,
    kernel_f, kernel_b, xp, xst, sst, acc, actz, bricks, send, recv, slz, hx, hy, hc, gwacc, red, rp, p0, r1, p1, r2, piece, p3, fin,
    halo_send, halo_recv, shalo_send, shalo_recv, cot_send, cot_recv, act_send, act_recv,
    s1_send, s1_recv, s2_send, s2_recv, s3_send, s3_recv, s4_send, s4_recv, pair_sem, local_sem,
):
    gx = lax.axis_index("gx")
    gy = lax.axis_index("gy")
    gz = gy // 4
    gyy = gy % 4

    def ring_peer(n):
        dz, dy = PEERS[n]
        return ((gz + dz) % 4) * 4 + (gyy + dy) % 4

    def side(n, sign):
        dx, dy = SIDES[n]
        return ((gx + GX + sign * dx) % GX, (gy + GY + sign * dy) % GY)

    barrier = pltpu.get_barrier_semaphore()
    for n in range(15):
        pl.semaphore_signal(barrier, inc=1, device_id=(gx, ring_peer(n)), device_id_type=MESH)
    for d in range(1, GX):
        pl.semaphore_signal(barrier, inc=1, device_id=((gx + d) % GX, gy), device_id_type=MESH)
    for h in range(GY):
        if h:
            pl.semaphore_signal(
                barrier, inc=1, device_id=((gx + 2) % GX, (gy + h) % GY), device_id_type=MESH
            )
    for n in range(4, 8):
        pl.semaphore_signal(barrier, inc=1, device_id=side(n, 1), device_id_type=MESH)

    lane = lax.broadcasted_iota(jnp.int32, (C, NZ), 1)

    def mask_row(x, y):
        return jnp.broadcast_to(mask[x, pl.ds(y, 1)].astype(f32), (C, NZ))

    def masked(x, _):
        for y in range(NY):
            xp[x + 1, y + 1] = (feat[x, y].astype(f32) * mask_row(x, y)).astype(bf16)
        return 0

    lax.fori_loop(0, NX, masked, 0)
    pl.semaphore_wait(barrier, 41)

    def span(d, sign):
        if d == 0:
            return pl.ds(1, 8)
        if sign > 0:
            return 8 if d > 0 else 1
        return 0 if d > 0 else 9

    halos = []
    for n, (dx, dy) in enumerate(SIDES):
        halos.append(
            pltpu.make_async_remote_copy(
                src_ref=xp.at[span(dx, 1), span(dy, 1)],
                dst_ref=xp.at[span(dx, -1), span(dy, -1)],
                send_sem=halo_send.at[n],
                recv_sem=halo_recv.at[n],
                device_id=side(n, 1),
                device_id_type=MESH,
            )
        )
    for copy in halos:
        copy.start()

    def cot_copy(n, k):
        peer = ring_peer(n)
        return pltpu.make_async_remote_copy(
            src_ref=cot_hbm.at[0, 2 * peer + k],
            dst_ref=recv.at[2 * gy + k],
            send_sem=cot_send.at[15 * k + n],
            recv_sem=cot_recv.at[15 * k + n],
            device_id=(gx, peer),
            device_id_type=MESH,
        )

    cots = [cot_copy(n, k) for k in range(2) for n in range(15)]
    for copy in cots:
        copy.start()
    own_cot = pltpu.make_async_copy(
        cot_hbm.at[0, pl.ds(2 * gy, 2)], recv.at[pl.ds(2 * gy, 2)], local_sem.at[0]
    )
    own_cot.start()

    for a in range(3):
        kernel_f[C * a : C * a + C] = jnp.concatenate([weight[a, b] for b in range(3)], axis=1)
        blocks = []
        for b in range(3):
            turned = jnp.transpose(weight[2 - a, 2 - b].astype(f32))
            for c in range(3):
                blocks.append(turned[(2 - c) * C : (3 - c) * C].astype(bf16))
        kernel_b[C * a : C * a + C] = jnp.concatenate(blocks, axis=1)

    owner = [owners[0, 0, z] for z in range(16)]
    slots = []
    for z in range(16):
        rank = jnp.int32(0)
        for before in range(z):
            rank = rank + (owner[before] == owner[z]).astype(jnp.int32)
        slots.append(2 * owner[z] + rank)

    def stack_inner(x, _):
        for y in range(NY):
            put_stack(xst, x + 1, y + 1, xp[x + 1, y + 1], lane)
        return 0

    lax.fori_loop(0, NX, stack_inner, 0)
    for copy in halos:
        copy.wait()

    first_x = (gx > 0).astype(f32)
    last_x = (gx < GX - 1).astype(f32)
    first_y = (gy > 0).astype(f32)
    last_y = (gy < GY - 1).astype(f32)

    def keep(tile, flag):
        return (tile.astype(f32) * flag).astype(bf16)

    def stack_y(x, _):
        put_stack(xst, x, 0, keep(xp[x, 0], first_y), lane)
        put_stack(xst, x, 9, keep(xp[x, 9], last_y), lane)
        return 0

    lax.fori_loop(1, 9, stack_y, 0)

    def stack_x(y, _):
        put_stack(xst, 0, y, keep(xp[0, y], first_x), lane)
        put_stack(xst, 9, y, keep(xp[9, y], last_x), lane)
        return 0

    lax.fori_loop(1, 9, stack_x, 0)
    for x, y, flag in (
        (0, 0, first_x * first_y), (0, 9, first_x * last_y),
        (9, 0, last_x * first_y), (9, 9, last_x * last_y),
    ):
        put_stack(xst, x, y, keep(xp[x, y], flag), lane)

    acc[0] = jnp.zeros((C, NY * NZ), f32)
    acc[1] = jnp.zeros((C, NY * NZ), f32)

    def forward(xi, _):
        conv_step(xi, kernel_f, xst, acc)
        return 0

    lax.fori_loop(0, NX + 2, forward, 0)

    shift = jnp.transpose(jnp.broadcast_to(bias[...], (NZ, C)))

    def activate(x, _):
        for y in range(NY):
            cols = slice(NZ * y, NZ * y + NZ)
            pre = acc[x + 2, :, cols] + shift
            gate = jax.nn.sigmoid(pre)
            on = mask_row(x, y)
            actz[x, :, cols] = (on * pre * gate).astype(bf16)
            acc[x + 2, :, cols] = on * gate * (1.0 + pre * (1.0 - gate))
        return 0

    lax.fori_loop(0, NX, activate, 0)
    bricks[16] = jnp.zeros((C, 512), bf16)

    def to_bricks(n, _):
        u2 = n // 2
        rows = pl.ds(pl.multiple_of((n % 2) * 48, 48), 48)
        cols = pl.ds(pl.multiple_of(u2 * NZ, NZ), NZ)
        tiles = [actz[2 * u2 + j // 8, rows, (j % 8) * NZ : (j % 8) * NZ + NZ] for j in range(16)]
        for z, tile in enumerate(swap_blocks(tiles)):
            bricks[z, rows, cols] = tile
        return 0

    lax.fori_loop(0, 8, to_bricks, 0)

    def fill(s, _):
        brick = jnp.int32(16)
        for z in range(16):
            brick = jnp.where(slots[z] == s, z, brick)
        send[s] = bricks[brick]
        return 0

    lax.fori_loop(0, SLOTS, fill, 0)

    for n in range(2):
        slz[n] = jnp.zeros((C, NY * NZ), bf16)
        slz[10 + n] = jnp.zeros((C, NY * NZ), bf16)

    own_cot.wait()
    for copy in cots:
        copy.wait()

    def act_copy(n, k):
        peer = ring_peer(n)
        return pltpu.make_async_remote_copy(
            src_ref=send.at[2 * peer + k],
            dst_ref=act_hbm.at[0, 2 * gy + k],
            send_sem=act_send.at[15 * k + n],
            recv_sem=act_recv.at[15 * k + n],
            device_id=(gx, peer),
            device_id_type=MESH,
        )

    acts = [act_copy(n, k) for k in range(2) for n in range(15)]
    own_act = pltpu.make_async_copy(
        send.at[pl.ds(2 * gy, 2)], act_hbm.at[0, pl.ds(2 * gy, 2)], local_sem.at[1]
    )
    own_act.start()
    for copy in acts[:4]:
        copy.start()

    def to_slope(n, _):
        u2 = n // 2
        rows = pl.ds(pl.multiple_of((n % 2) * 48, 48), 48)
        cols = pl.ds(pl.multiple_of(u2 * NZ, NZ), NZ)
        tiles = [recv[slots[z], rows, cols] for z in range(16)]
        for j, tile in enumerate(swap_blocks(tiles)):
            part = slice((j % 8) * NZ, (j % 8) * NZ + NZ)
            row = 2 * u2 + j // 8 + 2
            slz[row, rows, part] = (tile.astype(f32) * acc[row, rows, part]).astype(bf16)
        return 0

    lax.fori_loop(0, 8, to_slope, 0)

    def edge(d):
        return 9 if d > 0 else 2

    def strip(d):
        return pl.ds(7 * NZ, NZ) if d > 0 else pl.ds(0, NZ)

    def low(d):
        return 0 if d > 0 else 1

    slope_halos = []
    for n, (dx, dy) in enumerate(SIDES):
        if dy == 0:
            source, target = slz.at[edge(dx)], hx.at[low(dx)]
        elif dx == 0:
            source, target = slz.at[pl.ds(2, 8), :, strip(dy)], hy.at[low(dy)]
        else:
            source, target = slz.at[edge(dx), :, strip(dy)], hc.at[2 * low(dx) + low(dy)]
        slope_halos.append(
            pltpu.make_async_remote_copy(
                src_ref=source,
                dst_ref=target,
                send_sem=shalo_send.at[n],
                recv_sem=shalo_recv.at[n],
                device_id=side(n, 1),
                device_id_type=MESH,
            )
        )
    for copy in slope_halos:
        copy.start()
    for copy in acts[4:]:
        copy.start()

    gwacc[...] = jnp.zeros((K3, 7 * NZ), f32)

    def weight_terms(xi, _):
        left = jnp.concatenate([slz[xi + 2], slz[xi + 1], slz[xi]], axis=0)
        rows = xst[xi].reshape((NY + 2) * K3, NZ)
        right = jnp.concatenate([rows[K3 * y : K3 * y + K9] for y in range(NY)], axis=1)
        gwacc[:, 0:K9] += lax.dot_general(
            left, right, (((1,), (1,)), ((), ())), preferred_element_type=f32
        )
        return 0

    lax.fori_loop(0, 5, weight_terms, 0)
    lax.fori_loop(5, NX + 2, weight_terms, 0)
    for j in range(7):
        red[K3 * j : K3 * j + K3] = gwacc[:, NZ * j : NZ * j + NZ]
    red[7 * K3 : 2048] = jnp.zeros((2048 - 7 * K3, NZ), f32)

    cx = gx // 2
    core = gx % 2
    partner = cx * 2 + 1 - core
    half = pl.ds(pl.multiple_of(1024 * core, 1024), 1024)

    def chip(d):
        return ((cx + d) % 4) * 2 + core

    pair = pltpu.make_async_remote_copy(
        src_ref=red.at[pl.ds(1024 * (1 - core), 1024)],
        dst_ref=rp,
        send_sem=pair_sem.at[0],
        recv_sem=pair_sem.at[1],
        device_id=(partner, gy),
        device_id_type=MESH,
    )
    pair.start()

    def slope_inner(x, _):
        for y in range(NY):
            put_stack(sst, x + 1, y + 1, slz[x + 2, :, NZ * y : NZ * y + NZ], lane)
        return 0

    lax.fori_loop(0, NX, slope_inner, 0)
    pair.wait()
    p0[...] = red[half] + rp[...]

    def stage1(d):
        return pltpu.make_async_remote_copy(
            src_ref=p0.at[pl.ds(256 * ((cx + d) % 4), 256)],
            dst_ref=r1.at[d - 1],
            send_sem=s1_send.at[d],
            recv_sem=s1_recv.at[d],
            device_id=(chip(d), gy),
            device_id_type=MESH,
        )

    ones = [stage1(d) for d in range(1, 4)]
    for copy in ones:
        copy.start()
    for copy in slope_halos:
        copy.wait()

    def slope_y(x, _):
        put_stack(sst, x + 1, 0, keep(hy[0, x], first_y), lane)
        put_stack(sst, x + 1, 9, keep(hy[1, x], last_y), lane)
        return 0

    lax.fori_loop(0, NX, slope_y, 0)
    for y in range(NY):
        cols = slice(NZ * y, NZ * y + NZ)
        put_stack(sst, 0, y + 1, keep(hx[0, :, cols], first_x), lane)
        put_stack(sst, 9, y + 1, keep(hx[1, :, cols], last_x), lane)
    for n, x, y, flag in (
        (0, 0, 0, first_x * first_y), (1, 0, 9, first_x * last_y),
        (2, 9, 0, last_x * first_y), (3, 9, 9, last_x * last_y),
    ):
        put_stack(sst, x, y, keep(hc[n], flag), lane)

    def backward(xi, _):
        conv_step(xi, kernel_b, sst, acc)
        return 0

    lax.fori_loop(0, 3, backward, 0)

    for copy in ones:
        copy.wait()
    p1[...] = p0[pl.ds(pl.multiple_of(256 * cx, 256), 256)] + r1[0] + r1[1] + r1[2]

    beside = (gx + 2) % GX

    def stage2(n):
        peer = (gy + n) % GY
        return pltpu.make_async_remote_copy(
            src_ref=p1.at[pl.ds(16 * peer, 16)],
            dst_ref=r2.at[gy],
            send_sem=s2_send.at[n],
            recv_sem=s2_recv.at[n],
            device_id=(beside, peer),
            device_id_type=MESH,
        )

    twos = [stage2(n) for n in range(GY)]
    for copy in twos:
        copy.start()
    lax.fori_loop(3, 6, backward, 0)
    for copy in twos:
        copy.wait()
    part = r2[0]
    for n in range(1, GY):
        part = part + r2[n]
    piece[...] = part * TOTAL_SCALE
    mine = pl.ds(16 * gy, 16)

    def stage3(n):
        return pltpu.make_async_remote_copy(
            src_ref=piece,
            dst_ref=p3.at[mine],
            send_sem=s3_send.at[n],
            recv_sem=s3_recv.at[n],
            device_id=(beside, (gy + n) % GY),
            device_id_type=MESH,
        )

    threes = [stage3(n) for n in range(GY)]
    for copy in threes:
        copy.start()
    lax.fori_loop(6, 8, backward, 0)
    for copy in threes:
        copy.wait()

    block = pl.ds(pl.multiple_of(1024 * core + 256 * ((cx + 2) % 4), 256), 256)

    def stage4(d):
        return pltpu.make_async_remote_copy(
            src_ref=p3,
            dst_ref=fin.at[block],
            send_sem=s4_send.at[d],
            recv_sem=s4_recv.at[d],
            device_id=(chip(d), gy),
            device_id_type=MESH,
        )

    fours = [stage4(d) for d in range(1, 4)]
    for copy in fours:
        copy.start()
    fin[block] = p3[...]
    lax.fori_loop(8, NX + 2, backward, 0)

    def finish(x, _):
        for y in range(NY):
            gf_out[x, y] = (mask_row(x, y) * acc[x + 2, :, NZ * y : NZ * y + NZ]).astype(bf16)
        return 0

    lax.fori_loop(0, NX, finish, 0)
    for copy in fours:
        copy.wait()
    back = pltpu.make_async_remote_copy(
        src_ref=fin.at[half],
        dst_ref=fin.at[half],
        send_sem=pair_sem.at[2],
        recv_sem=pair_sem.at[3],
        device_id=(partner, gy),
        device_id_type=MESH,
    )
    back.start()
    back.wait()
    full = jnp.concatenate([fin[K3 * j : K3 * j + K3] for j in range(7)], axis=1)
    for a in range(3):
        for b in range(3):
            gw_out[a, b] = full[C * a : C * a + C, K3 * b : K3 * b + K3]
    own_act.wait()
    for copy in acts:
        copy.wait()


def hand_over(act, gf, gw, act_out, gf_out, gw_out, sems):
    pieces = [(act, act_out, (0, pl.ds(4 * n, 4))) for n in range(8)]
    pieces += [(gf, gf_out, (pl.ds(2 * n, 2),)) for n in range(4)]
    pieces += [(gw, gw_out, (n,)) for n in range(3)]
    copies = [
        pltpu.make_async_copy(source.at[part], target.at[part], sems.at[n])
        for n, (source, target, part) in enumerate(pieces)
    ]
    for copy in copies:
        copy.start()
    for copy in copies:
        copy.wait()


def on_device(features, active_mask, owners, weight, channel_bias, cotangent):
    smem = pl.BlockSpec(memory_space=pltpu.SMEM)
    vmem = pl.BlockSpec(memory_space=pltpu.VMEM)
    hbm = pl.BlockSpec(memory_space=pl.ANY)
    dma = pltpu.SemaphoreType.DMA
    activations, grad_features, grad = pl.pallas_call(
        body,
        out_shape=(
            pltpu.VMEM((1, SLOTS, C, 512), bf16),
            pltpu.VMEM((NX, NY, C, NZ), bf16),
            pltpu.VMEM((3, 3, C, K3), f32),
        ),
        in_specs=[smem, vmem, vmem, vmem, vmem, hbm],
        out_specs=(vmem, vmem, vmem),
        scratch_shapes=[
            pltpu.VMEM((K3, K9), bf16),
            pltpu.VMEM((K3, K9), bf16),
            pltpu.VMEM((NX + 2, NY + 2, C, NZ), bf16),
            pltpu.VMEM((NX + 2, NY + 2, K3, NZ), bf16),
            pltpu.VMEM((NX + 2, NY + 2, K3, NZ), bf16),
            pltpu.VMEM((NX + 4, C, NY * NZ), f32),
            pltpu.VMEM((NX, C, NY * NZ), bf16),
            pltpu.VMEM((17, C, 512), bf16),
            pltpu.VMEM((SLOTS, C, 512), bf16),
            pltpu.VMEM((SLOTS, C, 512), bf16),
            pltpu.VMEM((NX + 4, C, NY * NZ), bf16),
            pltpu.VMEM((2, C, NY * NZ), bf16),
            pltpu.VMEM((2, NX, C, NZ), bf16),
            pltpu.VMEM((4, C, NZ), bf16),
            pltpu.VMEM((K3, 7 * NZ), f32),
            pltpu.VMEM((2048, NZ), f32),
            pltpu.VMEM((1024, NZ), f32),
            pltpu.VMEM((1024, NZ), f32),
            pltpu.VMEM((3, 256, NZ), f32),
            pltpu.VMEM((256, NZ), f32),
            pltpu.VMEM((GY, 16, NZ), f32),
            pltpu.VMEM((16, NZ), f32),
            pltpu.VMEM((256, NZ), f32),
            pltpu.VMEM((2048, NZ), f32),
            dma((8,)), dma((8,)), dma((8,)), dma((8,)),
            dma((30,)), dma((30,)), dma((30,)), dma((30,)),
            dma((4,)), dma((4,)), dma((GY,)), dma((GY,)),
            dma((GY,)), dma((GY,)), dma((4,)), dma((4,)),
            dma((4,)), dma((2,)),
        ],
        compiler_params=pltpu.CompilerParams(
            collective_id=0, has_side_effects=True, vmem_limit_bytes=52 * 1024 * 1024
        ),
    )(owners, features, active_mask, weight, channel_bias.reshape(1, C), cotangent)
    return pl.pallas_call(
        hand_over,
        out_shape=(
            jax.ShapeDtypeStruct((1, SLOTS, C, 512), bf16),
            jax.ShapeDtypeStruct((NX, NY, C, NZ), bf16),
            jax.ShapeDtypeStruct((3, 3, C, K3), f32),
        ),
        in_specs=[vmem, vmem, vmem],
        out_specs=(hbm, hbm, hbm),
        scratch_shapes=[
            dma((15,)),
        ],
        compiler_params=pltpu.CompilerParams(vmem_limit_bytes=1024 * 1024),
    )(*(pltpu.with_memory_space_constraint(r, pltpu.VMEM) for r in (activations, grad_features, grad)))


def solution(mesh):
    in_specs = (
        P("gx", "gy", None, None),
        P("gx", "gy", None),
        P("gx", "gy", None),
        P(),
        P(),
        P("gx", "gy", None, None),
    )
    out_specs = (P("gx", "gy", None, None), P("gx", "gy", None, None), P())
    return jax.shard_map(
        on_device, mesh=mesh, in_specs=in_specs, out_specs=out_specs, check_vma=False
    )
```

```python
import jax
import jax.numpy as jnp
from jax import lax
from jax.experimental import pallas as pl
from jax.experimental.pallas import tpu as pltpu
from jax.sharding import PartitionSpec as P

C = 96
NX = 8
NY = 8
NZ = 128
GX = 8
GY = 16
SLOTS = 32
K3 = 3 * C
K9 = 9 * C
TOTAL_SCALE = (NX * NY * NZ * GX * GY) ** -0.5
f32 = jnp.float32
bf16 = jnp.bfloat16
MESH = pl.DeviceIdType.MESH

PEERS = (
    (1, 1), (3, 3), (1, 3), (3, 1), (0, 1), (0, 3), (1, 0), (3, 0),
    (2, 1), (2, 3), (1, 2), (3, 2), (2, 2), (0, 2), (2, 0),
)
SIDES = ((1, 0), (-1, 0), (0, 1), (0, -1), (1, 1), (1, -1), (-1, 1), (-1, -1))


def swap_blocks(tiles):
    lane = lax.broadcasted_iota(jnp.int32, tiles[0].shape, 1)
    for step in (8, 4, 2, 1):
        width = step * 8
        upper = (lane // width) % 2 == 1
        moved = list(tiles)
        for i in range(16):
            if i & step:
                continue
            j = i | step
            low, high = tiles[i], tiles[j]
            moved[i] = jnp.where(upper, pltpu.roll(high, width, 1), low)
            moved[j] = jnp.where(upper, high, pltpu.roll(low, NZ - width, 1))
        tiles = moved
    return tiles


def put_stack(stack, x, y, tile, lane):
    zero = jnp.zeros_like(tile)
    stack[x, y, 0:C] = jnp.where(lane == 0, zero, pltpu.roll(tile, 1, 1))
    stack[x, y, C : 2 * C] = tile
    stack[x, y, 2 * C : K3] = jnp.where(lane == NZ - 1, zero, pltpu.roll(tile, NZ - 1, 1))


def conv_step(xi, kernel, stack, acc):
    rows = stack[xi].reshape((NY + 2) * K3, NZ)
    right = jnp.concatenate([rows[K3 * y : K3 * y + K9] for y in range(NY)], axis=1)
    product = jnp.dot(kernel[...], right, preferred_element_type=f32)
    acc[xi + 2] = product[0:C]
    acc[xi + 1] += product[C : 2 * C]
    acc[xi] += product[2 * C : K3]


def body(
    owners, feat, mask, weight, bias, cot_hbm,
    act_hbm, gf_out, gw_out,
    kernel_f, kernel_b, xp, xst, sst, acc, actz, bricks, send, recv, slz, hx, hy, hc, gwacc, red, rp, p0, r1, p1, r2, piece, p3, fin,
    halo_send, halo_recv, shalo_send, shalo_recv, cot_send, cot_recv, act_send, act_recv,
    s1_send, s1_recv, s2_send, s2_recv, s3_send, s3_recv, s4_send, s4_recv, pair_sem, local_sem,
):
    gx = lax.axis_index("gx")
    gy = lax.axis_index("gy")
    gz = gy // 4
    gyy = gy % 4

    def ring_peer(n):
        dz, dy = PEERS[n]
        return ((gz + dz) % 4) * 4 + (gyy + dy) % 4

    def side(n, sign):
        dx, dy = SIDES[n]
        return ((gx + GX + sign * dx) % GX, (gy + GY + sign * dy) % GY)

    barrier = pltpu.get_barrier_semaphore()
    for n in range(15):
        pl.semaphore_signal(barrier, inc=1, device_id=(gx, ring_peer(n)), device_id_type=MESH)
    for d in range(1, GX):
        pl.semaphore_signal(barrier, inc=1, device_id=((gx + d) % GX, gy), device_id_type=MESH)
    for h in range(GY):
        if h:
            pl.semaphore_signal(
                barrier, inc=1, device_id=((gx + 2) % GX, (gy + h) % GY), device_id_type=MESH
            )
    for n in range(4, 8):
        pl.semaphore_signal(barrier, inc=1, device_id=side(n, 1), device_id_type=MESH)

    lane = lax.broadcasted_iota(jnp.int32, (C, NZ), 1)

    def mask_row(x, y):
        return jnp.broadcast_to(mask[x, pl.ds(y, 1)].astype(f32), (C, NZ))

    def masked(x, _):
        for y in range(NY):
            xp[x + 1, y + 1] = (feat[x, y].astype(f32) * mask_row(x, y)).astype(bf16)
        return 0

    lax.fori_loop(0, NX, masked, 0)
    pl.semaphore_wait(barrier, 41)

    def span(d, sign):
        if d == 0:
            return pl.ds(1, 8)
        if sign > 0:
            return 8 if d > 0 else 1
        return 0 if d > 0 else 9

    halos = []
    for n, (dx, dy) in enumerate(SIDES):
        halos.append(
            pltpu.make_async_remote_copy(
                src_ref=xp.at[span(dx, 1), span(dy, 1)],
                dst_ref=xp.at[span(dx, -1), span(dy, -1)],
                send_sem=halo_send.at[n],
                recv_sem=halo_recv.at[n],
                device_id=side(n, 1),
                device_id_type=MESH,
            )
        )
    for copy in halos:
        copy.start()

    def cot_copy(n, k):
        peer = ring_peer(n)
        return pltpu.make_async_remote_copy(
            src_ref=cot_hbm.at[0, 2 * peer + k],
            dst_ref=recv.at[2 * gy + k],
            send_sem=cot_send.at[15 * k + n],
            recv_sem=cot_recv.at[15 * k + n],
            device_id=(gx, peer),
            device_id_type=MESH,
        )

    cots = [cot_copy(n, k) for k in range(2) for n in range(15)]
    for copy in cots:
        copy.start()
    own_cot = pltpu.make_async_copy(
        cot_hbm.at[0, pl.ds(2 * gy, 2)], recv.at[pl.ds(2 * gy, 2)], local_sem.at[0]
    )
    own_cot.start()

    for a in range(3):
        kernel_f[C * a : C * a + C] = jnp.concatenate([weight[a, b] for b in range(3)], axis=1)
        blocks = []
        for b in range(3):
            turned = jnp.transpose(weight[2 - a, 2 - b].astype(f32))
            for c in range(3):
                blocks.append(turned[(2 - c) * C : (3 - c) * C].astype(bf16))
        kernel_b[C * a : C * a + C] = jnp.concatenate(blocks, axis=1)

    owner = [owners[0, 0, z] for z in range(16)]
    slots = []
    for z in range(16):
        rank = jnp.int32(0)
        for before in range(z):
            rank = rank + (owner[before] == owner[z]).astype(jnp.int32)
        slots.append(2 * owner[z] + rank)

    def stack_inner(x, _):
        for y in range(NY):
            put_stack(xst, x + 1, y + 1, xp[x + 1, y + 1], lane)
        return 0

    lax.fori_loop(0, NX, stack_inner, 0)
    for copy in halos:
        copy.wait()

    first_x = (gx > 0).astype(f32)
    last_x = (gx < GX - 1).astype(f32)
    first_y = (gy > 0).astype(f32)
    last_y = (gy < GY - 1).astype(f32)

    def keep(tile, flag):
        return (tile.astype(f32) * flag).astype(bf16)

    def stack_y(x, _):
        put_stack(xst, x, 0, keep(xp[x, 0], first_y), lane)
        put_stack(xst, x, 9, keep(xp[x, 9], last_y), lane)
        return 0

    lax.fori_loop(1, 9, stack_y, 0)

    def stack_x(y, _):
        put_stack(xst, 0, y, keep(xp[0, y], first_x), lane)
        put_stack(xst, 9, y, keep(xp[9, y], last_x), lane)
        return 0

    lax.fori_loop(1, 9, stack_x, 0)
    for x, y, flag in (
        (0, 0, first_x * first_y), (0, 9, first_x * last_y),
        (9, 0, last_x * first_y), (9, 9, last_x * last_y),
    ):
        put_stack(xst, x, y, keep(xp[x, y], flag), lane)

    acc[0] = jnp.zeros((C, NY * NZ), f32)
    acc[1] = jnp.zeros((C, NY * NZ), f32)

    def forward(xi, _):
        conv_step(xi, kernel_f, xst, acc)
        return 0

    lax.fori_loop(0, NX + 2, forward, 0)

    shift = jnp.transpose(jnp.broadcast_to(bias[...], (NZ, C)))

    def activate(x, _):
        for y in range(NY):
            cols = slice(NZ * y, NZ * y + NZ)
            pre = acc[x + 2, :, cols] + shift
            gate = jax.nn.sigmoid(pre)
            on = mask_row(x, y)
            actz[x, :, cols] = (on * pre * gate).astype(bf16)
            acc[x + 2, :, cols] = on * gate * (1.0 + pre * (1.0 - gate))
        return 0

    lax.fori_loop(0, NX, activate, 0)
    bricks[16] = jnp.zeros((C, 512), bf16)

    def to_bricks(u2, _):
        cols = pl.ds(pl.multiple_of(u2 * NZ, NZ), NZ)
        tiles = [actz[2 * u2 + j // 8, :, (j % 8) * NZ : (j % 8) * NZ + NZ] for j in range(16)]
        for z, tile in enumerate(swap_blocks(tiles)):
            bricks[z, :, cols] = tile
        return 0

    lax.fori_loop(0, 4, to_bricks, 0)

    def fill(s, _):
        brick = jnp.int32(16)
        for z in range(16):
            brick = jnp.where(slots[z] == s, z, brick)
        send[s] = bricks[brick]
        return 0

    lax.fori_loop(0, SLOTS, fill, 0)

    def act_copy(n, k):
        peer = ring_peer(n)
        return pltpu.make_async_remote_copy(
            src_ref=send.at[2 * peer + k],
            dst_ref=act_hbm.at[0, 2 * gy + k],
            send_sem=act_send.at[15 * k + n],
            recv_sem=act_recv.at[15 * k + n],
            device_id=(gx, peer),
            device_id_type=MESH,
        )

    acts = [act_copy(n, k) for k in range(2) for n in range(15)]
    own_act = pltpu.make_async_copy(
        send.at[pl.ds(2 * gy, 2)], act_hbm.at[0, pl.ds(2 * gy, 2)], local_sem.at[1]
    )
    own_act.start()
    for copy in acts[:6]:
        copy.start()

    for n in range(2):
        slz[n] = jnp.zeros((C, NY * NZ), bf16)
        slz[10 + n] = jnp.zeros((C, NY * NZ), bf16)

    own_cot.wait()
    for copy in cots:
        copy.wait()

    for copy in acts[6:8]:
        copy.start()

    def to_slope(u2, _):
        cols = pl.ds(pl.multiple_of(u2 * NZ, NZ), NZ)
        tiles = [recv[slots[z], :, cols] for z in range(16)]
        for j, tile in enumerate(swap_blocks(tiles)):
            part = slice((j % 8) * NZ, (j % 8) * NZ + NZ)
            row = 2 * u2 + j // 8 + 2
            slz[row, :, part] = (tile.astype(f32) * acc[row, :, part]).astype(bf16)
        return 0

    lax.fori_loop(0, 4, to_slope, 0)

    def edge(d):
        return 9 if d > 0 else 2

    def strip(d):
        return pl.ds(7 * NZ, NZ) if d > 0 else pl.ds(0, NZ)

    def low(d):
        return 0 if d > 0 else 1

    slope_halos = []
    for n, (dx, dy) in enumerate(SIDES):
        if dy == 0:
            source, target = slz.at[edge(dx)], hx.at[low(dx)]
        elif dx == 0:
            source, target = slz.at[pl.ds(2, 8), :, strip(dy)], hy.at[low(dy)]
        else:
            source, target = slz.at[edge(dx), :, strip(dy)], hc.at[2 * low(dx) + low(dy)]
        slope_halos.append(
            pltpu.make_async_remote_copy(
                src_ref=source,
                dst_ref=target,
                send_sem=shalo_send.at[n],
                recv_sem=shalo_recv.at[n],
                device_id=side(n, 1),
                device_id_type=MESH,
            )
        )
    for copy in slope_halos:
        copy.start()
    for copy in acts[8:]:
        copy.start()

    gwacc[...] = jnp.zeros((K3, 7 * NZ), f32)

    def weight_terms(xi, _):
        left = jnp.concatenate([slz[xi + 2], slz[xi + 1], slz[xi]], axis=0)
        rows = xst[xi].reshape((NY + 2) * K3, NZ)
        right = jnp.concatenate([rows[K3 * y : K3 * y + K9] for y in range(NY)], axis=1)
        gwacc[:, 0:K9] += lax.dot_general(
            left, right, (((1,), (1,)), ((), ())), preferred_element_type=f32
        )
        return 0

    lax.fori_loop(0, 5, weight_terms, 0)
    lax.fori_loop(5, NX + 2, weight_terms, 0)
    for j in range(7):
        red[K3 * j : K3 * j + K3] = gwacc[:, NZ * j : NZ * j + NZ]
    red[7 * K3 : 2048] = jnp.zeros((2048 - 7 * K3, NZ), f32)

    cx = gx // 2
    core = gx % 2
    partner = cx * 2 + 1 - core
    half = pl.ds(pl.multiple_of(1024 * core, 1024), 1024)

    def chip(d):
        return ((cx + d) % 4) * 2 + core

    pair = pltpu.make_async_remote_copy(
        src_ref=red.at[pl.ds(1024 * (1 - core), 1024)],
        dst_ref=rp,
        send_sem=pair_sem.at[0],
        recv_sem=pair_sem.at[1],
        device_id=(partner, gy),
        device_id_type=MESH,
    )
    pair.start()

    def slope_inner(x, _):
        for y in range(NY):
            put_stack(sst, x + 1, y + 1, slz[x + 2, :, NZ * y : NZ * y + NZ], lane)
        return 0

    lax.fori_loop(0, 4, slope_inner, 0)
    pair.wait()
    p0[...] = red[half] + rp[...]

    def stage1(d):
        return pltpu.make_async_remote_copy(
            src_ref=p0.at[pl.ds(256 * ((cx + d) % 4), 256)],
            dst_ref=r1.at[d - 1],
            send_sem=s1_send.at[d],
            recv_sem=s1_recv.at[d],
            device_id=(chip(d), gy),
            device_id_type=MESH,
        )

    ones = [stage1(d) for d in range(1, 4)]
    for copy in ones:
        copy.start()
    lax.fori_loop(4, NX, slope_inner, 0)

    def backward(xi, _):
        conv_step(xi, kernel_b, sst, acc)
        return 0

    for copy in ones:
        copy.wait()
    p1[...] = p0[pl.ds(pl.multiple_of(256 * cx, 256), 256)] + r1[0] + r1[1] + r1[2]

    beside = (gx + 2) % GX

    def stage2(n):
        peer = (gy + n) % GY
        return pltpu.make_async_remote_copy(
            src_ref=p1.at[pl.ds(16 * peer, 16)],
            dst_ref=r2.at[gy],
            send_sem=s2_send.at[n],
            recv_sem=s2_recv.at[n],
            device_id=(beside, peer),
            device_id_type=MESH,
        )

    twos = [stage2(n) for n in range(GY)]
    for copy in twos:
        copy.start()
    for copy in slope_halos:
        copy.wait()

    def slope_y(x, _):
        put_stack(sst, x + 1, 0, keep(hy[0, x], first_y), lane)
        put_stack(sst, x + 1, 9, keep(hy[1, x], last_y), lane)
        return 0

    lax.fori_loop(0, NX, slope_y, 0)
    for y in range(NY):
        cols = slice(NZ * y, NZ * y + NZ)
        put_stack(sst, 0, y + 1, keep(hx[0, :, cols], first_x), lane)
        put_stack(sst, 9, y + 1, keep(hx[1, :, cols], last_x), lane)
    for n, x, y, flag in (
        (0, 0, 0, first_x * first_y), (1, 0, 9, first_x * last_y),
        (2, 9, 0, last_x * first_y), (3, 9, 9, last_x * last_y),
    ):
        put_stack(sst, x, y, keep(hc[n], flag), lane)

    lax.fori_loop(0, 2, backward, 0)
    for copy in twos:
        copy.wait()
    part = r2[0]
    for n in range(1, GY):
        part = part + r2[n]
    piece[...] = (part * TOTAL_SCALE).astype(bf16)
    mine = pl.ds(16 * gy, 16)

    def stage3(n):
        return pltpu.make_async_remote_copy(
            src_ref=piece,
            dst_ref=p3.at[mine],
            send_sem=s3_send.at[n],
            recv_sem=s3_recv.at[n],
            device_id=(beside, (gy + n) % GY),
            device_id_type=MESH,
        )

    threes = [stage3(n) for n in range(GY)]
    for copy in threes:
        copy.start()
    lax.fori_loop(2, 6, backward, 0)
    for copy in threes:
        copy.wait()

    block = pl.ds(pl.multiple_of(1024 * core + 256 * ((cx + 2) % 4), 256), 256)

    def stage4(d):
        return pltpu.make_async_remote_copy(
            src_ref=p3,
            dst_ref=fin.at[block],
            send_sem=s4_send.at[d],
            recv_sem=s4_recv.at[d],
            device_id=(chip(d), gy),
            device_id_type=MESH,
        )

    fours = [stage4(d) for d in range(1, 4)]
    for copy in fours:
        copy.start()
    fin[block] = p3[...]
    lax.fori_loop(6, NX + 2, backward, 0)

    def finish(x, _):
        for y in range(NY):
            gf_out[x, y] = (mask_row(x, y) * acc[x + 2, :, NZ * y : NZ * y + NZ]).astype(bf16)
        return 0

    lax.fori_loop(0, NX, finish, 0)
    for copy in fours:
        copy.wait()
    back = pltpu.make_async_remote_copy(
        src_ref=fin.at[half],
        dst_ref=fin.at[half],
        send_sem=pair_sem.at[2],
        recv_sem=pair_sem.at[3],
        device_id=(partner, gy),
        device_id_type=MESH,
    )
    back.start()
    back.wait()
    full = jnp.concatenate(
        [fin[K3 * j : K3 * j + K3].astype(f32) for j in range(7)], axis=1
    )
    for a in range(3):
        for b in range(3):
            gw_out[a, b] = full[C * a : C * a + C, K3 * b : K3 * b + K3]
    own_act.wait()
    for copy in acts:
        copy.wait()


def hand_over(act, gf, gw, act_out, gf_out, gw_out, sems):
    pieces = [(act, act_out, (0, pl.ds(4 * n, 4))) for n in range(8)]
    pieces += [(gf, gf_out, (pl.ds(2 * n, 2),)) for n in range(4)]
    pieces += [(gw, gw_out, (n,)) for n in range(3)]
    copies = [
        pltpu.make_async_copy(source.at[part], target.at[part], sems.at[n])
        for n, (source, target, part) in enumerate(pieces)
    ]
    for copy in copies:
        copy.start()
    for copy in copies:
        copy.wait()


def on_device(features, active_mask, owners, weight, channel_bias, cotangent):
    smem = pl.BlockSpec(memory_space=pltpu.SMEM)
    vmem = pl.BlockSpec(memory_space=pltpu.VMEM)
    hbm = pl.BlockSpec(memory_space=pl.ANY)
    dma = pltpu.SemaphoreType.DMA
    activations, grad_features, grad = pl.pallas_call(
        body,
        out_shape=(
            pltpu.VMEM((1, SLOTS, C, 512), bf16),
            pltpu.VMEM((NX, NY, C, NZ), bf16),
            pltpu.VMEM((3, 3, C, K3), f32),
        ),
        in_specs=[smem, vmem, vmem, vmem, vmem, hbm],
        out_specs=(vmem, vmem, vmem),
        scratch_shapes=[
            pltpu.VMEM((K3, K9), bf16),
            pltpu.VMEM((K3, K9), bf16),
            pltpu.VMEM((NX + 2, NY + 2, C, NZ), bf16),
            pltpu.VMEM((NX + 2, NY + 2, K3, NZ), bf16),
            pltpu.VMEM((NX + 2, NY + 2, K3, NZ), bf16),
            pltpu.VMEM((NX + 4, C, NY * NZ), f32),
            pltpu.VMEM((NX, C, NY * NZ), bf16),
            pltpu.VMEM((17, C, 512), bf16),
            pltpu.VMEM((SLOTS, C, 512), bf16),
            pltpu.VMEM((SLOTS, C, 512), bf16),
            pltpu.VMEM((NX + 4, C, NY * NZ), bf16),
            pltpu.VMEM((2, C, NY * NZ), bf16),
            pltpu.VMEM((2, NX, C, NZ), bf16),
            pltpu.VMEM((4, C, NZ), bf16),
            pltpu.VMEM((K3, 7 * NZ), f32),
            pltpu.VMEM((2048, NZ), f32),
            pltpu.VMEM((1024, NZ), f32),
            pltpu.VMEM((1024, NZ), f32),
            pltpu.VMEM((3, 256, NZ), f32),
            pltpu.VMEM((256, NZ), f32),
            pltpu.VMEM((GY, 16, NZ), f32),
            pltpu.VMEM((16, NZ), bf16),
            pltpu.VMEM((256, NZ), bf16),
            pltpu.VMEM((2048, NZ), bf16),
            dma((8,)), dma((8,)), dma((8,)), dma((8,)),
            dma((30,)), dma((30,)), dma((30,)), dma((30,)),
            dma((4,)), dma((4,)), dma((GY,)), dma((GY,)),
            dma((GY,)), dma((GY,)), dma((4,)), dma((4,)),
            dma((4,)), dma((2,)),
        ],
        compiler_params=pltpu.CompilerParams(
            collective_id=0, has_side_effects=True, vmem_limit_bytes=52 * 1024 * 1024
        ),
    )(owners, features, active_mask, weight, channel_bias.reshape(1, C), cotangent)
    return pl.pallas_call(
        hand_over,
        out_shape=(
            jax.ShapeDtypeStruct((1, SLOTS, C, 512), bf16),
            jax.ShapeDtypeStruct((NX, NY, C, NZ), bf16),
            jax.ShapeDtypeStruct((3, 3, C, K3), f32),
        ),
        in_specs=[vmem, vmem, vmem],
        out_specs=(hbm, hbm, hbm),
        scratch_shapes=[
            dma((15,)),
        ],
        compiler_params=pltpu.CompilerParams(vmem_limit_bytes=1024 * 1024),
    )(*(pltpu.with_memory_space_constraint(r, pltpu.VMEM) for r in (activations, grad_features, grad)))


def solution(mesh):
    in_specs = (
        P("gx", "gy", None, None),
        P("gx", "gy", None),
        P("gx", "gy", None),
        P(),
        P(),
        P("gx", "gy", None, None),
    )
    out_specs = (P("gx", "gy", None, None), P("gx", "gy", None, None), P())
    return jax.shard_map(
        on_device, mesh=mesh, in_specs=in_specs, out_specs=out_specs, check_vma=False
    )
```

```python
import jax
import jax.numpy as jnp
from jax import lax
from jax.experimental import pallas as pl
from jax.experimental.pallas import tpu as pltpu
from jax.sharding import PartitionSpec as P

C = 96
NX = 8
NY = 8
NZ = 128
GX = 8
GY = 16
SLOTS = 32
K3 = 3 * C
K9 = 9 * C
TOTAL_SCALE = (NX * NY * NZ * GX * GY) ** -0.5
f32 = jnp.float32
bf16 = jnp.bfloat16
MESH = pl.DeviceIdType.MESH

PEERS = (
    (1, 1), (3, 3), (1, 3), (3, 1), (0, 1), (0, 3), (1, 0), (3, 0),
    (2, 1), (2, 3), (1, 2), (3, 2), (2, 2), (0, 2), (2, 0),
)
SIDES = ((1, 0), (-1, 0), (0, 1), (0, -1), (1, 1), (1, -1), (-1, 1), (-1, -1))


def swap_blocks(tiles):
    lane = lax.broadcasted_iota(jnp.int32, tiles[0].shape, 1)
    for step in (8, 4, 2, 1):
        width = step * 8
        upper = (lane // width) % 2 == 1
        moved = list(tiles)
        for i in range(16):
            if i & step:
                continue
            j = i | step
            low, high = tiles[i], tiles[j]
            moved[i] = jnp.where(upper, pltpu.roll(high, width, 1), low)
            moved[j] = jnp.where(upper, high, pltpu.roll(low, NZ - width, 1))
        tiles = moved
    return tiles


def put_stack(stack, x, y, tile, lane):
    zero = jnp.zeros_like(tile)
    stack[x, y, 0:C] = jnp.where(lane == 0, zero, pltpu.roll(tile, 1, 1))
    stack[x, y, C : 2 * C] = tile
    stack[x, y, 2 * C : K3] = jnp.where(lane == NZ - 1, zero, pltpu.roll(tile, NZ - 1, 1))


def conv_step(xi, kernel, stack, acc):
    rows = stack[xi].reshape((NY + 2) * K3, NZ)
    right = jnp.concatenate([rows[K3 * y : K3 * y + K9] for y in range(NY)], axis=1)
    product = jnp.dot(kernel[...], right, preferred_element_type=f32)
    acc[xi + 2] = product[0:C]
    acc[xi + 1] += product[C : 2 * C]
    acc[xi] += product[2 * C : K3]


def body(
    owners, feat_hbm, mask, weight, bias, cot_hbm,
    act_hbm, gf_out, gw_out,
    feat, kernel_f, kernel_b, xp, xst, sst, acc, actz, bricks, send, recv, slz, hx, hy, hc, gwacc, red, rp, p0, r1, p1, r2, piece, p3, fin,
    halo_send, halo_recv, shalo_send, shalo_recv, cot_send, cot_recv, act_send, act_recv,
    s1_send, s1_recv, s2_send, s2_recv, s3_send, s3_recv, s4_send, s4_recv, pair_sem, local_sem,
):
    gx = lax.axis_index("gx")
    gy = lax.axis_index("gy")
    gz = gy // 4
    gyy = gy % 4

    def ring_peer(n):
        dz, dy = PEERS[n]
        return ((gz + dz) % 4) * 4 + (gyy + dy) % 4

    def side(n, sign):
        dx, dy = SIDES[n]
        return ((gx + GX + sign * dx) % GX, (gy + GY + sign * dy) % GY)

    load = pltpu.make_async_copy(feat_hbm, feat, local_sem.at[2])
    load.start()
    barrier = pltpu.get_barrier_semaphore()
    for n in range(15):
        pl.semaphore_signal(barrier, inc=1, device_id=(gx, ring_peer(n)), device_id_type=MESH)
    for d in range(1, GX):
        pl.semaphore_signal(barrier, inc=1, device_id=((gx + d) % GX, gy), device_id_type=MESH)
    for h in range(GY):
        if h:
            pl.semaphore_signal(
                barrier, inc=1, device_id=((gx + 2) % GX, (gy + h) % GY), device_id_type=MESH
            )
    for n in range(4, 8):
        pl.semaphore_signal(barrier, inc=1, device_id=side(n, 1), device_id_type=MESH)

    pl.semaphore_wait(barrier, 41)

    def cot_copy(n, k):
        peer = ring_peer(n)
        return pltpu.make_async_remote_copy(
            src_ref=cot_hbm.at[0, 2 * peer + k],
            dst_ref=recv.at[2 * gy + k],
            send_sem=cot_send.at[15 * k + n],
            recv_sem=cot_recv.at[15 * k + n],
            device_id=(gx, peer),
            device_id_type=MESH,
        )

    cots = [cot_copy(n, k) for k in range(2) for n in range(15)]
    for copy in cots[:4]:
        copy.start()

    lane = lax.broadcasted_iota(jnp.int32, (C, NZ), 1)
    load.wait()

    def mask_row(x, y):
        return jnp.broadcast_to(mask[x, pl.ds(y, 1)].astype(f32), (C, NZ))

    def masked(x, _):
        for y in range(NY):
            xp[x + 1, y + 1] = (feat[x, y].astype(f32) * mask_row(x, y)).astype(bf16)
        return 0

    lax.fori_loop(0, NX, masked, 0)

    def span(d, sign):
        if d == 0:
            return pl.ds(1, 8)
        if sign > 0:
            return 8 if d > 0 else 1
        return 0 if d > 0 else 9

    halos = []
    for n, (dx, dy) in enumerate(SIDES):
        halos.append(
            pltpu.make_async_remote_copy(
                src_ref=xp.at[span(dx, 1), span(dy, 1)],
                dst_ref=xp.at[span(dx, -1), span(dy, -1)],
                send_sem=halo_send.at[n],
                recv_sem=halo_recv.at[n],
                device_id=side(n, 1),
                device_id_type=MESH,
            )
        )
    for copy in halos:
        copy.start()

    for copy in cots[4:]:
        copy.start()
    own_cot = pltpu.make_async_copy(
        cot_hbm.at[0, pl.ds(2 * gy, 2)], recv.at[pl.ds(2 * gy, 2)], local_sem.at[0]
    )
    own_cot.start()

    for a in range(3):
        kernel_f[C * a : C * a + C] = jnp.concatenate([weight[a, b] for b in range(3)], axis=1)
        blocks = []
        for b in range(3):
            turned = jnp.transpose(weight[2 - a, 2 - b].astype(f32))
            for c in range(3):
                blocks.append(turned[(2 - c) * C : (3 - c) * C].astype(bf16))
        kernel_b[C * a : C * a + C] = jnp.concatenate(blocks, axis=1)

    owner = [owners[0, 0, z] for z in range(16)]
    slots = []
    for z in range(16):
        rank = jnp.int32(0)
        for before in range(z):
            rank = rank + (owner[before] == owner[z]).astype(jnp.int32)
        slots.append(2 * owner[z] + rank)

    def stack_inner(x, _):
        for y in range(NY):
            put_stack(xst, x + 1, y + 1, xp[x + 1, y + 1], lane)
        return 0

    lax.fori_loop(0, NX, stack_inner, 0)
    for copy in halos:
        copy.wait()

    first_x = (gx > 0).astype(f32)
    last_x = (gx < GX - 1).astype(f32)
    first_y = (gy > 0).astype(f32)
    last_y = (gy < GY - 1).astype(f32)

    def keep(tile, flag):
        return (tile.astype(f32) * flag).astype(bf16)

    def stack_y(x, _):
        put_stack(xst, x, 0, keep(xp[x, 0], first_y), lane)
        put_stack(xst, x, 9, keep(xp[x, 9], last_y), lane)
        return 0

    lax.fori_loop(1, 9, stack_y, 0)

    def stack_x(y, _):
        put_stack(xst, 0, y, keep(xp[0, y], first_x), lane)
        put_stack(xst, 9, y, keep(xp[9, y], last_x), lane)
        return 0

    lax.fori_loop(1, 9, stack_x, 0)
    for x, y, flag in (
        (0, 0, first_x * first_y), (0, 9, first_x * last_y),
        (9, 0, last_x * first_y), (9, 9, last_x * last_y),
    ):
        put_stack(xst, x, y, keep(xp[x, y], flag), lane)

    acc[0] = jnp.zeros((C, NY * NZ), f32)
    acc[1] = jnp.zeros((C, NY * NZ), f32)

    def forward(xi, _):
        conv_step(xi, kernel_f, xst, acc)
        return 0

    lax.fori_loop(0, NX + 2, forward, 0)

    shift = jnp.transpose(jnp.broadcast_to(bias[...], (NZ, C)))

    def activate(x, _):
        for y in range(NY):
            cols = slice(NZ * y, NZ * y + NZ)
            pre = acc[x + 2, :, cols] + shift
            gate = jax.nn.sigmoid(pre)
            on = mask_row(x, y)
            actz[x, :, cols] = (on * pre * gate).astype(bf16)
            acc[x + 2, :, cols] = on * gate * (1.0 + pre * (1.0 - gate))
        return 0

    lax.fori_loop(0, NX, activate, 0)
    bricks[16] = jnp.zeros((C, 512), bf16)

    def to_bricks(u2, _):
        cols = pl.ds(pl.multiple_of(u2 * NZ, NZ), NZ)
        tiles = [actz[2 * u2 + j // 8, :, (j % 8) * NZ : (j % 8) * NZ + NZ] for j in range(16)]
        for z, tile in enumerate(swap_blocks(tiles)):
            bricks[z, :, cols] = tile
        return 0

    lax.fori_loop(0, 4, to_bricks, 0)

    def fill(s, _):
        brick = jnp.int32(16)
        for z in range(16):
            brick = jnp.where(slots[z] == s, z, brick)
        send[s] = bricks[brick]
        return 0

    lax.fori_loop(0, SLOTS, fill, 0)

    def act_copy(n, k):
        peer = ring_peer(n)
        return pltpu.make_async_remote_copy(
            src_ref=send.at[2 * peer + k],
            dst_ref=act_hbm.at[0, 2 * gy + k],
            send_sem=act_send.at[15 * k + n],
            recv_sem=act_recv.at[15 * k + n],
            device_id=(gx, peer),
            device_id_type=MESH,
        )

    acts = [act_copy(n, k) for k in range(2) for n in range(15)]
    own_act = pltpu.make_async_copy(
        send.at[pl.ds(2 * gy, 2)], act_hbm.at[0, pl.ds(2 * gy, 2)], local_sem.at[1]
    )
    own_act.start()
    for copy in acts[:2]:
        copy.start()

    for n in range(2):
        slz[n] = jnp.zeros((C, NY * NZ), bf16)
        slz[10 + n] = jnp.zeros((C, NY * NZ), bf16)

    own_cot.wait()
    for copy in cots:
        copy.wait()

    for copy in acts[2:6]:
        copy.start()

    def to_slope(u2, _):
        cols = pl.ds(pl.multiple_of(u2 * NZ, NZ), NZ)
        tiles = [recv[slots[z], :, cols] for z in range(16)]
        for j, tile in enumerate(swap_blocks(tiles)):
            part = slice((j % 8) * NZ, (j % 8) * NZ + NZ)
            row = 2 * u2 + j // 8 + 2
            slz[row, :, part] = (tile.astype(f32) * acc[row, :, part]).astype(bf16)
        return 0

    lax.fori_loop(0, 4, to_slope, 0)

    def edge(d):
        return 9 if d > 0 else 2

    def strip(d):
        return pl.ds(7 * NZ, NZ) if d > 0 else pl.ds(0, NZ)

    def low(d):
        return 0 if d > 0 else 1

    slope_halos = []
    for n, (dx, dy) in enumerate(SIDES):
        if dy == 0:
            source, target = slz.at[edge(dx)], hx.at[low(dx)]
        elif dx == 0:
            source, target = slz.at[pl.ds(2, 8), :, strip(dy)], hy.at[low(dy)]
        else:
            source, target = slz.at[edge(dx), :, strip(dy)], hc.at[2 * low(dx) + low(dy)]
        slope_halos.append(
            pltpu.make_async_remote_copy(
                src_ref=source,
                dst_ref=target,
                send_sem=shalo_send.at[n],
                recv_sem=shalo_recv.at[n],
                device_id=side(n, 1),
                device_id_type=MESH,
            )
        )
    for copy in slope_halos:
        copy.start()
    for copy in acts[6:]:
        copy.start()

    gwacc[...] = jnp.zeros((K3, 7 * NZ), f32)

    def weight_terms(xi, _):
        left = jnp.concatenate([slz[xi + 2], slz[xi + 1], slz[xi]], axis=0)
        rows = xst[xi].reshape((NY + 2) * K3, NZ)
        right = jnp.concatenate([rows[K3 * y : K3 * y + K9] for y in range(NY)], axis=1)
        gwacc[:, 0:K9] += lax.dot_general(
            left, right, (((1,), (1,)), ((), ())), preferred_element_type=f32
        )
        return 0

    lax.fori_loop(0, 5, weight_terms, 0)
    lax.fori_loop(5, NX + 2, weight_terms, 0)
    for j in range(7):
        red[K3 * j : K3 * j + K3] = gwacc[:, NZ * j : NZ * j + NZ]
    red[7 * K3 : 2048] = jnp.zeros((2048 - 7 * K3, NZ), f32)

    cx = gx // 2
    core = gx % 2
    partner = cx * 2 + 1 - core
    half = pl.ds(pl.multiple_of(1024 * core, 1024), 1024)

    def chip(d):
        return ((cx + d) % 4) * 2 + core

    pair = pltpu.make_async_remote_copy(
        src_ref=red.at[pl.ds(1024 * (1 - core), 1024)],
        dst_ref=rp,
        send_sem=pair_sem.at[0],
        recv_sem=pair_sem.at[1],
        device_id=(partner, gy),
        device_id_type=MESH,
    )
    pair.start()

    def slope_inner(x, _):
        for y in range(NY):
            put_stack(sst, x + 1, y + 1, slz[x + 2, :, NZ * y : NZ * y + NZ], lane)
        return 0

    lax.fori_loop(0, 4, slope_inner, 0)
    pair.wait()
    p0[...] = red[half] + rp[...]

    def stage1(d):
        return pltpu.make_async_remote_copy(
            src_ref=p0.at[pl.ds(256 * ((cx + d) % 4), 256)],
            dst_ref=r1.at[d - 1],
            send_sem=s1_send.at[d],
            recv_sem=s1_recv.at[d],
            device_id=(chip(d), gy),
            device_id_type=MESH,
        )

    ones = [stage1(d) for d in range(1, 4)]
    for copy in ones:
        copy.start()
    lax.fori_loop(4, NX, slope_inner, 0)

    def backward(xi, _):
        conv_step(xi, kernel_b, sst, acc)
        return 0

    for copy in ones:
        copy.wait()
    p1[...] = p0[pl.ds(pl.multiple_of(256 * cx, 256), 256)] + r1[0] + r1[1] + r1[2]

    beside = (gx + 2) % GX

    def stage2(n):
        peer = (gy + n) % GY
        return pltpu.make_async_remote_copy(
            src_ref=p1.at[pl.ds(16 * peer, 16)],
            dst_ref=r2.at[gy],
            send_sem=s2_send.at[n],
            recv_sem=s2_recv.at[n],
            device_id=(beside, peer),
            device_id_type=MESH,
        )

    twos = [stage2(n) for n in range(GY)]
    for copy in twos:
        copy.start()
    for copy in slope_halos:
        copy.wait()

    def slope_y(x, _):
        put_stack(sst, x + 1, 0, keep(hy[0, x], first_y), lane)
        put_stack(sst, x + 1, 9, keep(hy[1, x], last_y), lane)
        return 0

    lax.fori_loop(0, NX, slope_y, 0)
    for y in range(NY):
        cols = slice(NZ * y, NZ * y + NZ)
        put_stack(sst, 0, y + 1, keep(hx[0, :, cols], first_x), lane)
        put_stack(sst, 9, y + 1, keep(hx[1, :, cols], last_x), lane)
    for n, x, y, flag in (
        (0, 0, 0, first_x * first_y), (1, 0, 9, first_x * last_y),
        (2, 9, 0, last_x * first_y), (3, 9, 9, last_x * last_y),
    ):
        put_stack(sst, x, y, keep(hc[n], flag), lane)

    lax.fori_loop(0, 2, backward, 0)
    for copy in twos:
        copy.wait()
    part = r2[0]
    for n in range(1, GY):
        part = part + r2[n]
    piece[...] = (part * TOTAL_SCALE).astype(bf16)
    mine = pl.ds(16 * gy, 16)

    def stage3(n):
        return pltpu.make_async_remote_copy(
            src_ref=piece,
            dst_ref=p3.at[mine],
            send_sem=s3_send.at[n],
            recv_sem=s3_recv.at[n],
            device_id=(beside, (gy + n) % GY),
            device_id_type=MESH,
        )

    threes = [stage3(n) for n in range(GY)]
    for copy in threes:
        copy.start()
    lax.fori_loop(2, 6, backward, 0)
    for copy in threes:
        copy.wait()

    block = pl.ds(pl.multiple_of(1024 * core + 256 * ((cx + 2) % 4), 256), 256)

    def stage4(d):
        return pltpu.make_async_remote_copy(
            src_ref=p3,
            dst_ref=fin.at[block],
            send_sem=s4_send.at[d],
            recv_sem=s4_recv.at[d],
            device_id=(chip(d), gy),
            device_id_type=MESH,
        )

    fours = [stage4(d) for d in range(1, 4)]
    for copy in fours:
        copy.start()
    fin[block] = p3[...]
    lax.fori_loop(6, NX + 2, backward, 0)

    def finish(x, _):
        for y in range(NY):
            gf_out[x, y] = (mask_row(x, y) * acc[x + 2, :, NZ * y : NZ * y + NZ]).astype(bf16)
        return 0

    lax.fori_loop(0, NX, finish, 0)
    for copy in fours:
        copy.wait()
    back = pltpu.make_async_remote_copy(
        src_ref=fin.at[half],
        dst_ref=fin.at[half],
        send_sem=pair_sem.at[2],
        recv_sem=pair_sem.at[3],
        device_id=(partner, gy),
        device_id_type=MESH,
    )
    back.start()
    back.wait()
    full = jnp.concatenate(
        [fin[K3 * j : K3 * j + K3].astype(f32) for j in range(7)], axis=1
    )
    for a in range(3):
        for b in range(3):
            gw_out[a, b] = full[C * a : C * a + C, K3 * b : K3 * b + K3]
    own_act.wait()
    for copy in acts:
        copy.wait()


def hand_over(act, gf, gw, act_out, gf_out, gw_out, sems):
    pieces = [(act, act_out, (0, pl.ds(4 * n, 4))) for n in range(8)]
    pieces += [(gf, gf_out, (pl.ds(2 * n, 2),)) for n in range(4)]
    pieces += [(gw, gw_out, (n,)) for n in range(3)]
    copies = [
        pltpu.make_async_copy(source.at[part], target.at[part], sems.at[n])
        for n, (source, target, part) in enumerate(pieces)
    ]
    for copy in copies:
        copy.start()
    for copy in copies:
        copy.wait()


def on_device(features, active_mask, owners, weight, channel_bias, cotangent):
    smem = pl.BlockSpec(memory_space=pltpu.SMEM)
    vmem = pl.BlockSpec(memory_space=pltpu.VMEM)
    hbm = pl.BlockSpec(memory_space=pl.ANY)
    dma = pltpu.SemaphoreType.DMA
    activations, grad_features, grad = pl.pallas_call(
        body,
        out_shape=(
            pltpu.VMEM((1, SLOTS, C, 512), bf16),
            pltpu.VMEM((NX, NY, C, NZ), bf16),
            pltpu.VMEM((3, 3, C, K3), f32),
        ),
        in_specs=[smem, hbm, vmem, vmem, vmem, hbm],
        out_specs=(vmem, vmem, vmem),
        scratch_shapes=[
            pltpu.VMEM((NX, NY, C, NZ), bf16),
            pltpu.VMEM((K3, K9), bf16),
            pltpu.VMEM((K3, K9), bf16),
            pltpu.VMEM((NX + 2, NY + 2, C, NZ), bf16),
            pltpu.VMEM((NX + 2, NY + 2, K3, NZ), bf16),
            pltpu.VMEM((NX + 2, NY + 2, K3, NZ), bf16),
            pltpu.VMEM((NX + 4, C, NY * NZ), f32),
            pltpu.VMEM((NX, C, NY * NZ), bf16),
            pltpu.VMEM((17, C, 512), bf16),
            pltpu.VMEM((SLOTS, C, 512), bf16),
            pltpu.VMEM((SLOTS, C, 512), bf16),
            pltpu.VMEM((NX + 4, C, NY * NZ), bf16),
            pltpu.VMEM((2, C, NY * NZ), bf16),
            pltpu.VMEM((2, NX, C, NZ), bf16),
            pltpu.VMEM((4, C, NZ), bf16),
            pltpu.VMEM((K3, 7 * NZ), f32),
            pltpu.VMEM((2048, NZ), f32),
            pltpu.VMEM((1024, NZ), f32),
            pltpu.VMEM((1024, NZ), f32),
            pltpu.VMEM((3, 256, NZ), f32),
            pltpu.VMEM((256, NZ), f32),
            pltpu.VMEM((GY, 16, NZ), f32),
            pltpu.VMEM((16, NZ), bf16),
            pltpu.VMEM((256, NZ), bf16),
            pltpu.VMEM((2048, NZ), bf16),
            dma((8,)), dma((8,)), dma((8,)), dma((8,)),
            dma((30,)), dma((30,)), dma((30,)), dma((30,)),
            dma((4,)), dma((4,)), dma((GY,)), dma((GY,)),
            dma((GY,)), dma((GY,)), dma((4,)), dma((4,)),
            dma((4,)), dma((3,)),
        ],
        compiler_params=pltpu.CompilerParams(
            collective_id=0, has_side_effects=True, vmem_limit_bytes=52 * 1024 * 1024
        ),
    )(owners, features, active_mask, weight, channel_bias.reshape(1, C), cotangent)
    return pl.pallas_call(
        hand_over,
        out_shape=(
            jax.ShapeDtypeStruct((1, SLOTS, C, 512), bf16),
            jax.ShapeDtypeStruct((NX, NY, C, NZ), bf16),
            jax.ShapeDtypeStruct((3, 3, C, K3), f32),
        ),
        in_specs=[vmem, vmem, vmem],
        out_specs=(hbm, hbm, hbm),
        scratch_shapes=[
            dma((15,)),
        ],
        compiler_params=pltpu.CompilerParams(vmem_limit_bytes=1024 * 1024),
    )(*(pltpu.with_memory_space_constraint(r, pltpu.VMEM) for r in (activations, grad_features, grad)))


def solution(mesh):
    in_specs = (
        P("gx", "gy", None, None),
        P("gx", "gy", None),
        P("gx", "gy", None),
        P(),
        P(),
        P("gx", "gy", None, None),
    )
    out_specs = (P("gx", "gy", None, None), P("gx", "gy", None, None), P())
    return jax.shard_map(
        on_device, mesh=mesh, in_specs=in_specs, out_specs=out_specs, check_vma=False
    )
```

```python
import jax
import jax.numpy as jnp
from jax import lax
from jax.experimental import pallas as pl
from jax.experimental.pallas import tpu as pltpu
from jax.sharding import PartitionSpec as P

C = 96
NX = 8
NY = 8
NZ = 128
GX = 8
GY = 16
SLOTS = 32
K3 = 3 * C
K9 = 9 * C
TOTAL_SCALE = (NX * NY * NZ * GX * GY) ** -0.5
f32 = jnp.float32
bf16 = jnp.bfloat16
MESH = pl.DeviceIdType.MESH

PEERS = (
    (1, 1), (3, 3), (1, 3), (3, 1), (0, 1), (0, 3), (1, 0), (3, 0),
    (2, 1), (2, 3), (1, 2), (3, 2), (2, 2), (0, 2), (2, 0),
)
SIDES = ((1, 0), (-1, 0), (0, 1), (0, -1), (1, 1), (1, -1), (-1, 1), (-1, -1))


def swap_blocks(tiles):
    lane = lax.broadcasted_iota(jnp.int32, tiles[0].shape, 1)
    for step in (8, 4, 2, 1):
        width = step * 8
        upper = (lane // width) % 2 == 1
        moved = list(tiles)
        for i in range(16):
            if i & step:
                continue
            j = i | step
            low, high = tiles[i], tiles[j]
            moved[i] = jnp.where(upper, pltpu.roll(high, width, 1), low)
            moved[j] = jnp.where(upper, high, pltpu.roll(low, NZ - width, 1))
        tiles = moved
    return tiles


def put_stack(stack, x, y, tile, lane):
    zero = jnp.zeros_like(tile)
    stack[x, y, 0:C] = jnp.where(lane == 0, zero, pltpu.roll(tile, 1, 1))
    stack[x, y, C : 2 * C] = tile
    stack[x, y, 2 * C : K3] = jnp.where(lane == NZ - 1, zero, pltpu.roll(tile, NZ - 1, 1))


def conv_step(xi, kernel, stack, acc):
    rows = stack[xi].reshape((NY + 2) * K3, NZ)
    right = jnp.concatenate([rows[K3 * y : K3 * y + K9] for y in range(NY)], axis=1)
    product = jnp.dot(kernel[...], right, preferred_element_type=f32)
    acc[xi + 2] = product[0:C]
    acc[xi + 1] += product[C : 2 * C]
    acc[xi] += product[2 * C : K3]


def body(
    owners, feat_hbm, mask, weight, bias, cot_hbm,
    act_hbm, gf_out, gw_out,
    feat, kernel_f, kernel_b, xp, xst, sst, acc, actz, bricks, send, recv, slz, hx, hy, hc, gwacc, red, rp, p0, r1, p1, r2, piece, p3, fin,
    halo_send, halo_recv, shalo_send, shalo_recv, cot_send, cot_recv, act_send, act_recv,
    s1_send, s1_recv, s2_send, s2_recv, s3_send, s3_recv, s4_send, s4_recv, pair_sem, local_sem,
):
    gx = lax.axis_index("gx")
    gy = lax.axis_index("gy")
    gz = gy // 4
    gyy = gy % 4

    def ring_peer(n):
        dz, dy = PEERS[n]
        return ((gz + dz) % 4) * 4 + (gyy + dy) % 4

    def side(n, sign):
        dx, dy = SIDES[n]
        return ((gx + GX + sign * dx) % GX, (gy + GY + sign * dy) % GY)

    load = pltpu.make_async_copy(feat_hbm, feat, local_sem.at[2])
    load.start()
    barrier = pltpu.get_barrier_semaphore()
    for n in range(15):
        pl.semaphore_signal(barrier, inc=1, device_id=(gx, ring_peer(n)), device_id_type=MESH)
    for d in range(1, GX):
        pl.semaphore_signal(barrier, inc=1, device_id=((gx + d) % GX, gy), device_id_type=MESH)
    for h in range(GY):
        if h:
            pl.semaphore_signal(
                barrier, inc=1, device_id=((gx + 2) % GX, (gy + h) % GY), device_id_type=MESH
            )
    for n in range(4, 8):
        pl.semaphore_signal(barrier, inc=1, device_id=side(n, 1), device_id_type=MESH)

    pl.semaphore_wait(barrier, 41)

    def cot_copy(n, k):
        peer = ring_peer(n)
        return pltpu.make_async_remote_copy(
            src_ref=cot_hbm.at[0, 2 * peer + k],
            dst_ref=recv.at[2 * gy + k],
            send_sem=cot_send.at[15 * k + n],
            recv_sem=cot_recv.at[15 * k + n],
            device_id=(gx, peer),
            device_id_type=MESH,
        )

    cots = [cot_copy(n, k) for k in range(2) for n in range(15)]
    for copy in cots[:4]:
        copy.start()

    lane = lax.broadcasted_iota(jnp.int32, (C, NZ), 1)
    load.wait()

    def mask_row(x, y):
        return jnp.broadcast_to(mask[x, pl.ds(y, 1)].astype(f32), (C, NZ))

    def masked(x, _):
        for y in range(NY):
            xp[x + 1, y + 1] = (feat[x, y].astype(f32) * mask_row(x, y)).astype(bf16)
        return 0

    lax.fori_loop(0, NX, masked, 0)

    def span(d, sign):
        if d == 0:
            return pl.ds(1, 8)
        if sign > 0:
            return 8 if d > 0 else 1
        return 0 if d > 0 else 9

    halos = []
    for n, (dx, dy) in enumerate(SIDES):
        halos.append(
            pltpu.make_async_remote_copy(
                src_ref=xp.at[span(dx, 1), span(dy, 1)],
                dst_ref=xp.at[span(dx, -1), span(dy, -1)],
                send_sem=halo_send.at[n],
                recv_sem=halo_recv.at[n],
                device_id=side(n, 1),
                device_id_type=MESH,
            )
        )
    for copy in halos:
        copy.start()

    for copy in cots[4:]:
        copy.start()
    own_cot = pltpu.make_async_copy(
        cot_hbm.at[0, pl.ds(2 * gy, 2)], recv.at[pl.ds(2 * gy, 2)], local_sem.at[0]
    )
    own_cot.start()

    for a in range(3):
        kernel_f[C * a : C * a + C] = jnp.concatenate([weight[a, b] for b in range(3)], axis=1)
        blocks = []
        for b in range(3):
            turned = jnp.transpose(weight[2 - a, 2 - b].astype(f32))
            for c in range(3):
                blocks.append(turned[(2 - c) * C : (3 - c) * C].astype(bf16))
        kernel_b[C * a : C * a + C] = jnp.concatenate(blocks, axis=1)

    owner = [owners[0, 0, z] for z in range(16)]
    slots = []
    for z in range(16):
        rank = jnp.int32(0)
        for before in range(z):
            rank = rank + (owner[before] == owner[z]).astype(jnp.int32)
        slots.append(2 * owner[z] + rank)

    def stack_inner(x, _):
        for y in range(NY):
            put_stack(xst, x + 1, y + 1, xp[x + 1, y + 1], lane)
        return 0

    lax.fori_loop(0, NX, stack_inner, 0)
    for copy in halos:
        copy.wait()

    first_x = (gx > 0).astype(f32)
    last_x = (gx < GX - 1).astype(f32)
    first_y = (gy > 0).astype(f32)
    last_y = (gy < GY - 1).astype(f32)

    def keep(tile, flag):
        return (tile.astype(f32) * flag).astype(bf16)

    def stack_y(x, _):
        put_stack(xst, x, 0, keep(xp[x, 0], first_y), lane)
        put_stack(xst, x, 9, keep(xp[x, 9], last_y), lane)
        return 0

    lax.fori_loop(1, 9, stack_y, 0)

    def stack_x(y, _):
        put_stack(xst, 0, y, keep(xp[0, y], first_x), lane)
        put_stack(xst, 9, y, keep(xp[9, y], last_x), lane)
        return 0

    lax.fori_loop(1, 9, stack_x, 0)
    for x, y, flag in (
        (0, 0, first_x * first_y), (0, 9, first_x * last_y),
        (9, 0, last_x * first_y), (9, 9, last_x * last_y),
    ):
        put_stack(xst, x, y, keep(xp[x, y], flag), lane)

    acc[0] = jnp.zeros((C, NY * NZ), f32)
    acc[1] = jnp.zeros((C, NY * NZ), f32)

    def forward(xi, _):
        conv_step(xi, kernel_f, xst, acc)
        return 0

    lax.fori_loop(0, NX + 2, forward, 0)

    shift = jnp.transpose(jnp.broadcast_to(bias[...], (NZ, C)))

    def activate(x, _):
        for y in range(NY):
            cols = slice(NZ * y, NZ * y + NZ)
            pre = acc[x + 2, :, cols] + shift
            gate = jax.nn.sigmoid(pre)
            on = mask_row(x, y)
            actz[x, :, cols] = (on * pre * gate).astype(bf16)
            acc[x + 2, :, cols] = on * gate * (1.0 + pre * (1.0 - gate))
        return 0

    lax.fori_loop(0, NX, activate, 0)
    bricks[16] = jnp.zeros((C, 512), bf16)

    def to_bricks(u2, _):
        cols = pl.ds(pl.multiple_of(u2 * NZ, NZ), NZ)
        tiles = [actz[2 * u2 + j // 8, :, (j % 8) * NZ : (j % 8) * NZ + NZ] for j in range(16)]
        for z, tile in enumerate(swap_blocks(tiles)):
            bricks[z, :, cols] = tile
        return 0

    lax.fori_loop(0, 4, to_bricks, 0)

    def fill(s, _):
        brick = jnp.int32(16)
        for z in range(16):
            brick = jnp.where(slots[z] == s, z, brick)
        send[s] = bricks[brick]
        return 0

    lax.fori_loop(0, SLOTS, fill, 0)

    def act_copy(n, k):
        peer = ring_peer(n)
        return pltpu.make_async_remote_copy(
            src_ref=send.at[2 * peer + k],
            dst_ref=act_hbm.at[0, 2 * gy + k],
            send_sem=act_send.at[15 * k + n],
            recv_sem=act_recv.at[15 * k + n],
            device_id=(gx, peer),
            device_id_type=MESH,
        )

    acts = [act_copy(n, k) for k in range(2) for n in range(15)]
    own_act = pltpu.make_async_copy(
        send.at[pl.ds(2 * gy, 2)], act_hbm.at[0, pl.ds(2 * gy, 2)], local_sem.at[1]
    )
    own_act.start()
    for copy in acts[:2]:
        copy.start()

    for n in range(2):
        slz[n] = jnp.zeros((C, NY * NZ), bf16)
        slz[10 + n] = jnp.zeros((C, NY * NZ), bf16)

    own_cot.wait()
    for copy in cots:
        copy.wait()

    for copy in acts[2:6]:
        copy.start()

    def to_slope(u2, _):
        cols = pl.ds(pl.multiple_of(u2 * NZ, NZ), NZ)
        tiles = [recv[slots[z], :, cols] for z in range(16)]
        for j, tile in enumerate(swap_blocks(tiles)):
            part = slice((j % 8) * NZ, (j % 8) * NZ + NZ)
            row = 2 * u2 + j // 8 + 2
            slz[row, :, part] = (tile.astype(f32) * acc[row, :, part]).astype(bf16)
        return 0

    lax.fori_loop(0, 4, to_slope, 0)

    def edge(d):
        return 9 if d > 0 else 2

    def strip(d):
        return pl.ds(7 * NZ, NZ) if d > 0 else pl.ds(0, NZ)

    def low(d):
        return 0 if d > 0 else 1

    slope_halos = []
    for n, (dx, dy) in enumerate(SIDES):
        if dy == 0:
            source, target = slz.at[edge(dx)], hx.at[low(dx)]
        elif dx == 0:
            source, target = slz.at[pl.ds(2, 8), :, strip(dy)], hy.at[low(dy)]
        else:
            source, target = slz.at[edge(dx), :, strip(dy)], hc.at[2 * low(dx) + low(dy)]
        slope_halos.append(
            pltpu.make_async_remote_copy(
                src_ref=source,
                dst_ref=target,
                send_sem=shalo_send.at[n],
                recv_sem=shalo_recv.at[n],
                device_id=side(n, 1),
                device_id_type=MESH,
            )
        )
    for n in (2, 3, 4, 5, 6, 7, 0, 1):
        slope_halos[n].start()

    gwacc[...] = jnp.zeros((K3, 7 * NZ), f32)

    def weight_terms(xi, _):
        left = jnp.concatenate([slz[xi + 2], slz[xi + 1], slz[xi]], axis=0)
        rows = xst[xi].reshape((NY + 2) * K3, NZ)
        right = jnp.concatenate([rows[K3 * y : K3 * y + K9] for y in range(NY)], axis=1)
        gwacc[:, 0:K9] += lax.dot_general(
            left, right, (((1,), (1,)), ((), ())), preferred_element_type=f32
        )
        return 0

    lax.fori_loop(0, 5, weight_terms, 0)
    for copy in acts[6:]:
        copy.start()
    lax.fori_loop(5, NX + 2, weight_terms, 0)
    for j in range(7):
        red[K3 * j : K3 * j + K3] = gwacc[:, NZ * j : NZ * j + NZ]
    red[7 * K3 : 2048] = jnp.zeros((2048 - 7 * K3, NZ), f32)

    cx = gx // 2
    core = gx % 2
    partner = cx * 2 + 1 - core
    half = pl.ds(pl.multiple_of(1024 * core, 1024), 1024)

    def chip(d):
        return ((cx + d) % 4) * 2 + core

    pair = pltpu.make_async_remote_copy(
        src_ref=red.at[pl.ds(1024 * (1 - core), 1024)],
        dst_ref=rp,
        send_sem=pair_sem.at[0],
        recv_sem=pair_sem.at[1],
        device_id=(partner, gy),
        device_id_type=MESH,
    )
    pair.start()

    def slope_inner(x, _):
        for y in range(NY):
            put_stack(sst, x + 1, y + 1, slz[x + 2, :, NZ * y : NZ * y + NZ], lane)
        return 0

    lax.fori_loop(0, 4, slope_inner, 0)
    pair.wait()
    p0[...] = red[half] + rp[...]

    def stage1(d):
        return pltpu.make_async_remote_copy(
            src_ref=p0.at[pl.ds(256 * ((cx + d) % 4), 256)],
            dst_ref=r1.at[d - 1],
            send_sem=s1_send.at[d],
            recv_sem=s1_recv.at[d],
            device_id=(chip(d), gy),
            device_id_type=MESH,
        )

    ones = [stage1(d) for d in range(1, 4)]
    for copy in ones:
        copy.start()
    lax.fori_loop(4, NX, slope_inner, 0)

    def backward(xi, _):
        conv_step(xi, kernel_b, sst, acc)
        return 0

    for copy in ones:
        copy.wait()
    p1[...] = p0[pl.ds(pl.multiple_of(256 * cx, 256), 256)] + r1[0] + r1[1] + r1[2]

    beside = (gx + 2) % GX

    def stage2(n):
        peer = (gy + n) % GY
        return pltpu.make_async_remote_copy(
            src_ref=p1.at[pl.ds(16 * peer, 16)],
            dst_ref=r2.at[gy],
            send_sem=s2_send.at[n],
            recv_sem=s2_recv.at[n],
            device_id=(beside, peer),
            device_id_type=MESH,
        )

    twos = [stage2(n) for n in range(GY)]
    for copy in twos:
        copy.start()
    for copy in slope_halos:
        copy.wait()

    def slope_y(x, _):
        put_stack(sst, x + 1, 0, keep(hy[0, x], first_y), lane)
        put_stack(sst, x + 1, 9, keep(hy[1, x], last_y), lane)
        return 0

    lax.fori_loop(0, NX, slope_y, 0)
    for y in range(NY):
        cols = slice(NZ * y, NZ * y + NZ)
        put_stack(sst, 0, y + 1, keep(hx[0, :, cols], first_x), lane)
        put_stack(sst, 9, y + 1, keep(hx[1, :, cols], last_x), lane)
    for n, x, y, flag in (
        (0, 0, 0, first_x * first_y), (1, 0, 9, first_x * last_y),
        (2, 9, 0, last_x * first_y), (3, 9, 9, last_x * last_y),
    ):
        put_stack(sst, x, y, keep(hc[n], flag), lane)

    lax.fori_loop(0, 2, backward, 0)
    for copy in twos:
        copy.wait()
    part = r2[0]
    for n in range(1, GY):
        part = part + r2[n]
    piece[...] = (part * TOTAL_SCALE).astype(bf16)
    mine = pl.ds(16 * gy, 16)

    def stage3(n):
        return pltpu.make_async_remote_copy(
            src_ref=piece,
            dst_ref=p3.at[mine],
            send_sem=s3_send.at[n],
            recv_sem=s3_recv.at[n],
            device_id=(beside, (gy + n) % GY),
            device_id_type=MESH,
        )

    threes = [stage3(n) for n in range(GY)]
    for copy in threes:
        copy.start()
    lax.fori_loop(2, 6, backward, 0)
    for copy in threes:
        copy.wait()

    block = pl.ds(pl.multiple_of(1024 * core + 256 * ((cx + 2) % 4), 256), 256)

    def stage4(d):
        return pltpu.make_async_remote_copy(
            src_ref=p3,
            dst_ref=fin.at[block],
            send_sem=s4_send.at[d],
            recv_sem=s4_recv.at[d],
            device_id=(chip(d), gy),
            device_id_type=MESH,
        )

    fours = [stage4(d) for d in range(1, 4)]
    for copy in fours:
        copy.start()
    fin[block] = p3[...]
    lax.fori_loop(6, NX + 2, backward, 0)

    def finish(x, _):
        for y in range(NY):
            gf_out[x, y] = (mask_row(x, y) * acc[x + 2, :, NZ * y : NZ * y + NZ]).astype(bf16)
        return 0

    lax.fori_loop(0, NX, finish, 0)
    for copy in fours:
        copy.wait()
    back = pltpu.make_async_remote_copy(
        src_ref=fin.at[half],
        dst_ref=fin.at[half],
        send_sem=pair_sem.at[2],
        recv_sem=pair_sem.at[3],
        device_id=(partner, gy),
        device_id_type=MESH,
    )
    back.start()
    back.wait()
    full = jnp.concatenate(
        [fin[K3 * j : K3 * j + K3].astype(f32) for j in range(7)], axis=1
    )
    for a in range(3):
        for b in range(3):
            gw_out[a, b] = full[C * a : C * a + C, K3 * b : K3 * b + K3]
    own_act.wait()
    for copy in acts:
        copy.wait()


def hand_over(act, gf, gw, act_out, gf_out, gw_out, sems):
    pieces = [(act, act_out, (0, pl.ds(4 * n, 4))) for n in range(8)]
    pieces += [(gf, gf_out, (pl.ds(2 * n, 2),)) for n in range(4)]
    pieces += [(gw, gw_out, (n,)) for n in range(3)]
    copies = [
        pltpu.make_async_copy(source.at[part], target.at[part], sems.at[n])
        for n, (source, target, part) in enumerate(pieces)
    ]
    for copy in copies:
        copy.start()
    for copy in copies:
        copy.wait()


def on_device(features, active_mask, owners, weight, channel_bias, cotangent):
    smem = pl.BlockSpec(memory_space=pltpu.SMEM)
    vmem = pl.BlockSpec(memory_space=pltpu.VMEM)
    hbm = pl.BlockSpec(memory_space=pl.ANY)
    dma = pltpu.SemaphoreType.DMA
    activations, grad_features, grad = pl.pallas_call(
        body,
        out_shape=(
            pltpu.VMEM((1, SLOTS, C, 512), bf16),
            pltpu.VMEM((NX, NY, C, NZ), bf16),
            pltpu.VMEM((3, 3, C, K3), f32),
        ),
        in_specs=[smem, hbm, vmem, vmem, vmem, hbm],
        out_specs=(vmem, vmem, vmem),
        scratch_shapes=[
            pltpu.VMEM((NX, NY, C, NZ), bf16),
            pltpu.VMEM((K3, K9), bf16),
            pltpu.VMEM((K3, K9), bf16),
            pltpu.VMEM((NX + 2, NY + 2, C, NZ), bf16),
            pltpu.VMEM((NX + 2, NY + 2, K3, NZ), bf16),
            pltpu.VMEM((NX + 2, NY + 2, K3, NZ), bf16),
            pltpu.VMEM((NX + 4, C, NY * NZ), f32),
            pltpu.VMEM((NX, C, NY * NZ), bf16),
            pltpu.VMEM((17, C, 512), bf16),
            pltpu.VMEM((SLOTS, C, 512), bf16),
            pltpu.VMEM((SLOTS, C, 512), bf16),
            pltpu.VMEM((NX + 4, C, NY * NZ), bf16),
            pltpu.VMEM((2, C, NY * NZ), bf16),
            pltpu.VMEM((2, NX, C, NZ), bf16),
            pltpu.VMEM((4, C, NZ), bf16),
            pltpu.VMEM((K3, 7 * NZ), f32),
            pltpu.VMEM((2048, NZ), f32),
            pltpu.VMEM((1024, NZ), f32),
            pltpu.VMEM((1024, NZ), f32),
            pltpu.VMEM((3, 256, NZ), f32),
            pltpu.VMEM((256, NZ), f32),
            pltpu.VMEM((GY, 16, NZ), f32),
            pltpu.VMEM((16, NZ), bf16),
            pltpu.VMEM((256, NZ), bf16),
            pltpu.VMEM((2048, NZ), bf16),
            dma((8,)), dma((8,)), dma((8,)), dma((8,)),
            dma((30,)), dma((30,)), dma((30,)), dma((30,)),
            dma((4,)), dma((4,)), dma((GY,)), dma((GY,)),
            dma((GY,)), dma((GY,)), dma((4,)), dma((4,)),
            dma((4,)), dma((3,)),
        ],
        compiler_params=pltpu.CompilerParams(
            collective_id=0, has_side_effects=True, vmem_limit_bytes=52 * 1024 * 1024
        ),
    )(owners, features, active_mask, weight, channel_bias.reshape(1, C), cotangent)
    return pl.pallas_call(
        hand_over,
        out_shape=(
            jax.ShapeDtypeStruct((1, SLOTS, C, 512), bf16),
            jax.ShapeDtypeStruct((NX, NY, C, NZ), bf16),
            jax.ShapeDtypeStruct((3, 3, C, K3), f32),
        ),
        in_specs=[vmem, vmem, vmem],
        out_specs=(hbm, hbm, hbm),
        scratch_shapes=[
            dma((15,)),
        ],
        compiler_params=pltpu.CompilerParams(vmem_limit_bytes=1024 * 1024),
    )(*(pltpu.with_memory_space_constraint(r, pltpu.VMEM) for r in (activations, grad_features, grad)))


def solution(mesh):
    in_specs = (
        P("gx", "gy", None, None),
        P("gx", "gy", None),
        P("gx", "gy", None),
        P(),
        P(),
        P("gx", "gy", None, None),
    )
    out_specs = (P("gx", "gy", None, None), P("gx", "gy", None, None), P())
    return jax.shard_map(
        on_device, mesh=mesh, in_specs=in_specs, out_specs=out_specs, check_vma=False
    )
```
